32 devices in a mesh: ctx: 16 (over z, y, x), head: 2 (over core), dp: 1.
Axes of the slice: x: 2, y: 2, z: 4, core: 2. Of those that a mesh axis runs over, the one named last changes fastest.
Arguments:
- queries: bfloat16 [2048, 4096], P(('dp', 'ctx'), 'head'), may hold values from -24 to 24
- key_rows: bfloat16 [2048, 1024], P(('dp', 'ctx'), 'head'), may hold values from -6 to 6
- value_rows: bfloat16 [2048, 1024], P(('dp', 'ctx'), 'head'), may hold values from -24 to 24
- grad_out: bfloat16 [2048, 4096], P(('dp', 'ctx'), 'head'), may hold values from -12 to 12
- doc_ids: int32 [2048], P(('dp', 'ctx')), may hold values from 0 to 4, never falling along the last dimension, each value on 1 to 1024 neighbouring positions
- loss_mask: int32 [2048], P(('dp', 'ctx')), may hold values from 0 to 1
- windows: int32 [32], P('head'), may hold values from 32 to 768, as said below
Outputs:
- attended: bfloat16 [2048, 4096], P(('dp', 'ctx'), 'head')
- grad_queries: bfloat16 [2048, 4096], P(('dp', 'ctx'), 'head')
- grad_keys: bfloat16 [2048, 1024], P(('dp', 'ctx'), 'head')
- grad_values: bfloat16 [2048, 1024], P(('dp', 'ctx'), 'head')
The draws below stay inside these ranges and needn't reach their ends.
Inputs may be any that keep to these rules, and one draw needn't show every extreme that they name: `windows`: some query head in every aligned group of 8 heads has the window 768.
All inputs are finite; a program needn't handle non-finite values.
Results may differ from the reference program's by a relative error of at most 0.0078.
Values may be sent and summed in bfloat16 or wider, within the bound.
No kernel may reach another device: no remote copies, remote signals or barrier semaphores. Data moves between devices by JAX's collectives and lax.ppermute only.
A program may use at most 64 MiB of HBM per device.

```python
import math
import jax
import jax.numpy as jnp
import numpy as np
from jax import lax

HEADS = 32
KV_HEADS = 8
HEAD_DIM = 128
WINDOW = 768
TOK_DEV = 128
HOPS = 6
TOKENS = 2048


def drawn_pair(key):
    key_vals = jnp.clip(jax.random.normal(jax.random.fold_in(key, 101), (TOKENS, KV_HEADS, HEAD_DIM), jnp.float32), -6.0, 6.0)
    query_vals = jnp.clip(jax.random.normal(jax.random.fold_in(key, 102), (TOKENS, HEADS, HEAD_DIM), jnp.float32), -6.0, 6.0)
    return (query_vals, key_vals)


def draw_queries(key, part):
    query_vals, key_vals = drawn_pair(key)
    return query_vals.reshape(TOKENS, HEADS * HEAD_DIM).astype(jnp.bfloat16)


def draw_key_rows(key, part):
    query_vals, key_vals = drawn_pair(key)
    return key_vals.reshape(TOKENS, KV_HEADS * HEAD_DIM).astype(jnp.bfloat16)


def draw_loss_mask(key, part):
    token_index = jnp.arange(TOKENS, dtype=jnp.int32)
    threshold = 200 + 400 * token_index // TOKENS
    drawn = jax.random.randint(jax.random.fold_in(key, 301), (TOKENS,), 0, 1000)
    return (drawn < threshold).astype(jnp.int32)


def draw_windows(key, part):
    lowest = WINDOW // 24
    drawn_lengths = jax.random.randint(jax.random.fold_in(key, 201), (HEADS,), lowest, WINDOW + 1)
    chosen_slot = jax.random.randint(jax.random.fold_in(key, 202), (), 0, 8)
    head_index = jnp.arange(HEADS)
    return jnp.where(head_index % 8 == chosen_slot, WINDOW, drawn_lengths).astype(jnp.int32)


def block_levels(stream_key, shape, pieces, low, top_value):
    level = 1.0
    for axis_at, parts in pieces:
        heights = jax.random.uniform(jax.random.fold_in(jax.random.fold_in(stream_key, 6), axis_at), (parts,), jnp.float32, low / len(pieces), top_value / len(pieces))
        level = level * jnp.repeat(jnp.exp(heights), shape[axis_at] // parts).reshape((-1,) + (1,) * (len(shape) - 1 - axis_at))
    return level


def length_profile(number_of, total, reach, lean):
    loads = [(1 << 20) // math.isqrt(standing ** lean) + 1 for standing in range(2, number_of + 1)]
    spare, counts = total - reach - (number_of - 1), [1] * (number_of - 1)
    while spare > 0:
        candidates = [i for i in range(number_of - 1) if counts[i] < reach]
        mass, budget = sum([loads[i] for i in candidates]), spare
        for i in candidates:
            more = min(reach - counts[i], max(1, budget * loads[i] // mass), spare)
            counts[i] = counts[i] + more
            spare = spare - more
    return np.array([reach] + counts)


def ragged(rng, amount, total, limit, lean):
    if amount == 2:
        one = jax.random.randint(rng, (), max(1, total - limit), min(limit, total - 1) + 1)
        return jnp.stack([one, total - one])
    lengths = jnp.asarray(length_profile(amount, total, limit, lean), jnp.int32)
    twos = (amount - 1) // 2
    source_of, receiver = lengths[1:1 + 2 * twos:2], lengths[2:2 + 2 * twos:2]
    margin = jnp.minimum(source_of - 1, limit - receiver)
    moved = jax.random.randint(jax.random.fold_in(rng, 1), (twos,), 0, 1 << 20) % (margin + 1)
    lengths = lengths.at[1:1 + 2 * twos:2].set(source_of - moved).at[2:2 + 2 * twos:2].set(receiver + moved)
    return lengths[jax.random.permutation(jax.random.fold_in(rng, 2), amount)]


def bell_draw(rng, dims, spread, most, pieces=(), kind=jnp.bfloat16):
    factor_of = block_levels(rng, dims, pieces, -0.22, 0.18) if pieces else 1.0
    result = jax.random.normal(rng, dims, jnp.float32) * spread * factor_of
    return jnp.minimum(jnp.maximum(result, -most), most).astype(kind)


def setup_inputs(seed: int = 0, part: int = 0) -> dict:
    arg_keys = jax.random.split(jax.random.key(seed), 8)
    part_keys = jax.random.split(jax.random.fold_in(arg_keys[7], part), 8)
    queries = draw_queries(jax.random.fold_in(jax.random.fold_in(arg_keys[7], part), 71), part)
    key_rows = draw_key_rows(jax.random.fold_in(jax.random.fold_in(arg_keys[7], part), 71), part)
    value_rows = bell_draw(part_keys[2], (TOKENS, KV_HEADS * HEAD_DIM), 4.0, 24.0, ((0, 16), (1, 2)))
    grad_out = bell_draw(part_keys[3], (TOKENS, HEADS * HEAD_DIM), 2.0, 12.0, ((0, 16), (1, 2)))
    doc_ids = jnp.searchsorted(jnp.cumsum(ragged(part_keys[4], TOKENS // (WINDOW // 2), TOKENS, min(3 * WINDOW, TOKENS // 2), 0)), jnp.arange(TOKENS), side="right").astype(jnp.int32)
    loss_mask = draw_loss_mask(jax.random.fold_in(jax.random.fold_in(arg_keys[7], part), 71), part)
    windows = draw_windows(jax.random.fold_in(arg_keys[7], 71), part)
    return {"queries": queries, "key_rows": key_rows, "value_rows": value_rows, "grad_out": grad_out, "doc_ids": doc_ids, "loss_mask": loss_mask, "windows": windows}


def round_low(values):
    lowered = lax.optimization_barrier(values.astype(jnp.bfloat16))
    return lowered.astype(jnp.float32)


def band_pass(query_blk, key_band, value_band, grad_blk, score_mask, score_scale):
    exact_mode = lax.Precision.HIGHEST
    scores = jnp.einsum("rhgd,khd->hgrk", query_blk, key_band, precision=exact_mode) * score_scale
    scores = jnp.where(score_mask, scores, -jnp.inf)
    row_max = jnp.max(scores, axis=-1, keepdims=True)
    raised = jnp.exp(scores - row_max)
    weights = raised / jnp.sum(raised, axis=-1, keepdims=True)
    weights_low = round_low(weights)
    output = jnp.einsum("hgrk,khd->rhgd", weights_low, value_band, precision=exact_mode)
    row_dot = jnp.sum(grad_blk * output, axis=-1)
    grad_prob = jnp.einsum("rhgd,khd->hgrk", grad_blk, value_band, precision=exact_mode)
    grad_score = round_low(weights * (grad_prob - jnp.transpose(row_dot, (1, 2, 0))[..., None]))
    grad_query = jnp.einsum("hgrk,khd->rhgd", grad_score, key_band, precision=exact_mode) * score_scale
    grad_key = jnp.einsum("hgrk,rhgd->khd", grad_score, query_blk, precision=exact_mode) * score_scale
    grad_value = jnp.einsum("hgrk,rhgd->khd", weights_low, grad_blk, precision=exact_mode)
    return output, grad_query, grad_key, grad_value


def reference(queries, key_rows, value_rows, grad_out, doc_ids, loss_mask, windows):
    group_size = HEADS // KV_HEADS
    block_count = TOKENS // TOK_DEV
    band_rows = (HOPS + 1) * TOK_DEV
    pad_rows = HOPS * TOK_DEV
    score_scale = HEAD_DIM ** -0.5
    mask_float = loss_mask.astype(jnp.float32)
    loss_count = jnp.sum(mask_float)
    factor = TOKENS / jnp.maximum(loss_count, 1.0)
    cotangent = ((grad_out.astype(jnp.float32) * mask_float[:, None]) * factor).astype(jnp.bfloat16)
    query_all = queries.astype(jnp.float32).reshape(TOKENS, KV_HEADS, group_size, HEAD_DIM)
    grad_all = cotangent.astype(jnp.float32).reshape(TOKENS, KV_HEADS, group_size, HEAD_DIM)
    key_all = key_rows.astype(jnp.float32).reshape(TOKENS, KV_HEADS, HEAD_DIM)
    value_all = value_rows.astype(jnp.float32).reshape(TOKENS, KV_HEADS, HEAD_DIM)
    zero_rows = jnp.zeros((pad_rows, KV_HEADS, HEAD_DIM), jnp.float32)
    key_pad = jnp.concatenate([zero_rows, key_all], axis=0)
    value_pad = jnp.concatenate([zero_rows, value_all], axis=0)
    doc_pad = jnp.concatenate([jnp.full((pad_rows,), -1, jnp.int32), doc_ids.astype(jnp.int32)], axis=0)
    head_reach = windows.astype(jnp.int32).reshape(KV_HEADS, group_size)[:, :, None, None]
    query_offsets = jnp.arange(TOK_DEV, dtype=jnp.int32)
    band_offsets = jnp.arange(band_rows, dtype=jnp.int32)

    def one_block(accum, block_index):
        key_acc, value_acc = accum
        block_start = (block_index * TOK_DEV).astype(jnp.int32)
        query_blk = lax.dynamic_slice_in_dim(query_all, block_start, TOK_DEV, 0)
        grad_blk = lax.dynamic_slice_in_dim(grad_all, block_start, TOK_DEV, 0)
        key_band = lax.dynamic_slice_in_dim(key_pad, block_start, band_rows, 0)
        value_band = lax.dynamic_slice_in_dim(value_pad, block_start, band_rows, 0)
        doc_query = lax.dynamic_slice_in_dim(doc_ids.astype(jnp.int32), block_start, TOK_DEV, 0)
        doc_band = lax.dynamic_slice_in_dim(doc_pad, block_start, band_rows, 0)
        query_pos = block_start + query_offsets
        key_pos = block_start - pad_rows + band_offsets
        distance = query_pos[:, None] - key_pos[None, :]
        admissible = (key_pos[None, :] >= 0) & (distance >= 0) & (doc_query[:, None] == doc_band[None, :])
        score_mask = admissible[None, None] & (distance[None, None] < head_reach)
        output, grad_query, grad_key, grad_value = band_pass(query_blk, key_band, value_band, grad_blk, score_mask, score_scale)
        key_old = lax.dynamic_slice_in_dim(key_acc, block_start, band_rows, 0)
        value_old = lax.dynamic_slice_in_dim(value_acc, block_start, band_rows, 0)
        key_acc = lax.dynamic_update_slice_in_dim(key_acc, key_old + grad_key, block_start, 0)
        value_acc = lax.dynamic_update_slice_in_dim(value_acc, value_old + grad_value, block_start, 0)
        return (key_acc, value_acc), (output.astype(jnp.bfloat16), grad_query.astype(jnp.bfloat16))

    start_acc = jnp.zeros((TOKENS + pad_rows, KV_HEADS, HEAD_DIM), jnp.float32)
    (key_acc, value_acc), (outputs, grad_queries) = lax.scan(one_block, (start_acc, start_acc), jnp.arange(block_count, dtype=jnp.int32))
    attended = outputs.reshape(TOKENS, HEADS * HEAD_DIM)
    grad_queries = grad_queries.reshape(TOKENS, HEADS * HEAD_DIM)
    grad_keys = key_acc[pad_rows:].reshape(TOKENS, KV_HEADS * HEAD_DIM).astype(jnp.bfloat16)
    grad_values = value_acc[pad_rows:].reshape(TOKENS, KV_HEADS * HEAD_DIM).astype(jnp.bfloat16)
    return (attended, grad_queries, grad_keys, grad_values)
```

```python
import functools

import jax
import jax.numpy as jnp
from jax import lax
from jax.experimental import pallas as pl
from jax.experimental.pallas import tpu as pltpu
from jax.sharding import PartitionSpec as P

HEAD_DIM = 128
WINDOW = 768
AXIS = "ctx"
PAD = 16
PAIR = 2
BF16 = jnp.bfloat16
F32 = jnp.float32
NEG = -1e30
NT = (((1,), (1,)), ((), ()))
NN = (((1,), (0,)), ((), ()))


def dot(a, b, dims=NN):
    return lax.dot_general(a, b, dims, preferred_element_type=F32)


def block_at(index, size):
    return pl.ds(pl.multiple_of(index * size, size), size)


def call(kernel, out_shape, scalars, vectors, scratch=(), flops=0, nbytes=0, vmem=None):
    return pl.pallas_call(
        kernel,
        out_shape=out_shape,
        in_specs=[pl.BlockSpec(memory_space=pltpu.SMEM)] * len(scalars)
        + [pl.BlockSpec(memory_space=pltpu.VMEM)] * len(vectors),
        out_specs=jax.tree.map(lambda _: pl.BlockSpec(memory_space=pltpu.VMEM), out_shape),
        scratch_shapes=list(scratch),
        cost_estimate=pl.CostEstimate(flops=flops, bytes_accessed=nbytes, transcendentals=0),
        compiler_params=pltpu.CompilerParams(vmem_limit_bytes=vmem),
    )(*scalars, *vectors)


def pack_kv_kernel(group, r_ref, key_ref, value_ref, doc_ref, mask_ref, *out_refs):
    r = r_ref[0]
    rows = key_ref.shape[0]
    line = jnp.concatenate([doc_ref[...].astype(F32), mask_ref[...].astype(F32)], axis=1)
    tail = jnp.broadcast_to(line, (PAD, 2 * HEAD_DIM)).astype(BF16)
    for j in range(group):
        cols = block_at(r ^ j, HEAD_DIM)
        out_refs[j][0:rows, 0:HEAD_DIM] = key_ref[:, cols]
        out_refs[j][0:rows, HEAD_DIM:] = value_ref[:, cols]
        out_refs[j][rows:, :] = tail


def pack_qg_kernel(group, r_ref, query_ref, grad_ref, *out_refs):
    r = r_ref[0]
    width = query_ref.shape[1] // group
    for j in range(group):
        cols = block_at(r ^ j, width)
        out_refs[j][:, 0:width] = query_ref[:, cols]
        out_refs[j][:, width:] = grad_ref[:, cols]


def gather_kernel(group, needs, r_ref, *refs):
    slots, outs = refs[:group], refs[group:]
    r = r_ref[0]
    full, count_ref = outs[0], outs[-1]
    rows = full.shape[1] - PAD
    total = jnp.zeros((1, HEAD_DIM), F32)
    for j in range(group):
        full[r ^ j] = slots[j][...]
        total = total + slots[j][rows : rows + 1, HEAD_DIM:].astype(F32)
    count_ref[...] = jnp.broadcast_to(jnp.sum(total, axis=1, keepdims=True), count_ref.shape)
    for need, out in zip([n for n in needs if n < group], outs[1:-1]):
        out[...] = full[group - need :]


def attention_kernel(
    group, needs, heads, token_count, r_ref, base_ref, window_ref, count_ref, own_ref, *refs
):
    halo_refs, refs = refs[: len(needs)], refs[len(needs) :]
    qg_refs, refs = refs[:group], refs[group:]
    out_refs, refs = refs[:group], refs[group:]
    own_out, refs = refs[0], refs[1:]
    halo_outs, refs = refs[: len(needs)], refs[len(needs) :]
    keys, values, keys_t, values_t, dkeys, dvalues, qg, od, lines = refs
    r = r_ref[0]
    rows = own_ref.shape[1] - PAD
    hops = sum(needs)
    blocks = hops + group
    span = (hops + 1) * rows
    width = heads * HEAD_DIM
    scale = HEAD_DIM**-0.5
    exp_scale = scale * 1.4426950408889634
    lowest = jnp.maximum(hops * rows - base_ref[0], 0)

    pieces = []
    for need, ref in reversed(list(zip(needs, halo_refs))):
        pieces += [(ref, i) for i in range(need)]
    pieces += [(own_ref, i) for i in range(group)]
    lines[...] = jnp.zeros_like(lines)
    factor = token_count / jnp.maximum(count_ref[0:1, :], 1.0)
    for kb, (ref, i) in enumerate(pieces):
        at = slice(kb * rows, (kb + 1) * rows)
        key, value = ref[i, 0:rows, 0:HEAD_DIM], ref[i, 0:rows, HEAD_DIM:]
        keys[at, :] = key
        values[at, :] = value
        keys_t[:, at] = key.T
        values_t[:, at] = value.T
        doc = ref[i, rows : rows + 1, 0:HEAD_DIM].astype(F32)
        if kb < hops:
            doc = jnp.where(kb * rows < lowest, -1.0, doc)
        else:
            s = kb - hops
            mask = ref[i, rows : rows + 1, HEAD_DIM:].astype(F32)
            lines[blocks + s : blocks + s + 1, :] = mask * factor
        lines[kb : kb + 1, :] = doc
    columns = lines[...].T
    dkeys[...] = jnp.zeros_like(dkeys)
    dvalues[...] = jnp.zeros_like(dvalues)
    for j in range(group):
        qg[r ^ j] = qg_refs[j][...]

    lane = lax.broadcasted_iota(jnp.int32, (1, rows), 1)
    pos = lax.broadcasted_iota(jnp.int32, (span, PAIR * rows), 0)
    diag = lax.broadcasted_iota(jnp.int32, (rows, PAIR * rows), 0)
    own_lane = jnp.concatenate([lane] * PAIR, axis=1)
    for s in range(group):
        at = slice(s * rows, s * rows + span)
        doc_row = lines[hops + s : hops + s + 1, :]
        start = jnp.zeros((1, rows), F32)
        for kb in range(s, s + hops + 1):
            before = jnp.where(columns[:, kb : kb + 1] < doc_row, 1.0, 0.0)
            start = start + jnp.sum(before, axis=0, keepdims=True)
        start = jnp.maximum(start.astype(jnp.int32), lowest - s * rows)
        cot_col = columns[:, blocks + s : blocks + s + 1]
        for h0 in range(0, heads, PAIR):
            hs = range(h0, h0 + PAIR)
            low = jnp.concatenate(
                [
                    jnp.maximum(start, hops * rows + 1 + lane - window_ref[r * heads + h])
                    for h in hs
                ],
                axis=1,
            )
            query = jnp.concatenate(
                [qg[s, :, h * HEAD_DIM : (h + 1) * HEAD_DIM] for h in hs], axis=0
            )
            cots = [
                qg[s, :, width + h * HEAD_DIM : width + (h + 1) * HEAD_DIM].astype(F32) * cot_col
                for h in hs
            ]
            cots = [c.astype(BF16) for c in cots]
            cot = jnp.concatenate(cots, axis=0)
            cot_t = jnp.concatenate([c.T for c in cots], axis=1).astype(F32)
            scores = dot(keys[at, :], query, NT)
            allowed = pos >= low
            scores = jnp.where(allowed, scores, NEG)
            last = jnp.where(diag <= own_lane, scores[hops * rows :], NEG)
            scores = jnp.concatenate([scores[: hops * rows], last], axis=0)
            row_max = jnp.max(scores, axis=0, keepdims=True)
            raised = jnp.exp2(scores * exp_scale - row_max * exp_scale)
            weights = raised * (1.0 / jnp.sum(raised, axis=0, keepdims=True))
            weights_low = weights.astype(BF16)
            output_t = dot(values_t[:, at], weights_low)
            row_dot = jnp.sum(cot_t * output_t, axis=0, keepdims=True)
            grad_prob = dot(values[at, :], cot, NT)
            grad_score = (weights * (grad_prob - row_dot)).astype(BF16)
            dvalues[at, :] += dot(weights_low, cot)
            dkeys[at, :] += dot(grad_score, query)
            grad_query_t = dot(keys_t[:, at], grad_score) * scale
            for i, h in enumerate(hs):
                cut = slice(i * rows, (i + 1) * rows)
                od[s, :, h * HEAD_DIM : (h + 1) * HEAD_DIM] = output_t[:, cut].T.astype(BF16)
                od[s, :, width + h * HEAD_DIM : width + (h + 1) * HEAD_DIM] = grad_query_t[
                    :, cut
                ].T.astype(BF16)

    for j in range(group):
        out_refs[j][...] = od[r ^ j]
    first = hops * rows
    own_out[:, 0:HEAD_DIM] = dkeys[first:, :]
    own_out[:, HEAD_DIM:] = dvalues[first:, :]
    for need, out in zip(needs, halo_outs):
        first -= need * rows
        out[:, 0:HEAD_DIM] = dkeys[first : first + need * rows, :].astype(BF16)
        out[:, HEAD_DIM:] = dvalues[first : first + need * rows, :].astype(BF16)


def add_kv_kernel(group, needs, r_ref, own_ref, *refs):
    halo_refs, out_refs, total = refs[: len(needs)], refs[len(needs) : -1], refs[-1]
    r = r_ref[0]
    rows = own_ref.shape[0] // group
    scale = HEAD_DIM**-0.5
    for s in range(group):
        part = own_ref[s * rows : (s + 1) * rows, :]
        for need, ref in zip(needs, halo_refs):
            i = s - (group - need)
            if i >= 0:
                part = part + ref[i * rows : (i + 1) * rows, :].astype(F32)
        total[s, :, 0:HEAD_DIM] = (part[:, 0:HEAD_DIM] * scale).astype(BF16)
        total[s, :, HEAD_DIM:] = part[:, HEAD_DIM:].astype(BF16)
    for j in range(group):
        out_refs[j][...] = total[r ^ j]


def unpack_kernel(group, r_ref, *refs):
    slots, (left_ref, right_ref) = refs[:group], refs[group:]
    r = r_ref[0]
    width = left_ref.shape[1] // group
    for j in range(group):
        cols = block_at(r ^ j, width)
        left_ref[:, cols] = slots[j][:, 0:width]
        right_ref[:, cols] = slots[j][:, width:]


def per_device(queries, key_rows, value_rows, grad_out, doc_ids, loss_mask, windows):
    count = lax.axis_size(AXIS)
    rows = key_rows.shape[0]
    group = key_rows.shape[1] // HEAD_DIM
    heads = queries.shape[1] // key_rows.shape[1]
    width = heads * HEAD_DIM
    assert rows == HEAD_DIM and count % group == 0 and group & (group - 1) == 0
    hops = (WINDOW - 1 + rows - 1) // rows
    needs = [min(group, hops - k) for k in range(0, hops, group)]
    blocks = hops + group
    index = lax.axis_index(AXIS)
    r = (index % group).reshape(1)
    base = ((index // group) * (group * rows)).reshape(1)
    shape = jax.ShapeDtypeStruct

    def swap(array, by):
        return lax.ppermute(array, AXIS, [(i, i ^ by) for i in range(count)])

    def shift(array, by):
        pairs = [(i, i + by) for i in range(count) if 0 <= i + by < count]
        return lax.ppermute(array, AXIS, pairs)

    message = shape((rows + PAD, 2 * HEAD_DIM), BF16)
    kv = call(
        functools.partial(pack_kv_kernel, group),
        [message] * group,
        [r],
        [key_rows, value_rows, doc_ids.reshape(1, rows), loss_mask.reshape(1, rows)],
    )
    kv = [kv[0]] + [swap(kv[j], j) for j in range(1, group)]
    qg = call(
        functools.partial(pack_qg_kernel, group),
        [shape((rows, 2 * width), BF16)] * group,
        [r],
        [queries, grad_out],
    )
    qg = [qg[0]] + [swap(qg[j], j) for j in range(1, group)]
    *held, counted = call(
        functools.partial(gather_kernel, group, needs),
        [shape((n, rows + PAD, 2 * HEAD_DIM), BF16) for n in [group] + [n for n in needs if n < group]]
        + [shape((8, HEAD_DIM), F32)],
        [r],
        kv,
    )
    parts = iter(held[1:])
    halo = [
        shift(held[0] if need == group else next(parts), group * (k + 1))
        for k, need in enumerate(needs)
    ]
    by = group
    while by < count:
        counted = counted + swap(counted, by)
        by *= 2

    vmem = pltpu.VMEM
    results = call(
        functools.partial(attention_kernel, group, needs, heads, float(count * rows)),
        [shape((rows, 2 * width), BF16)] * group
        + [shape((group * rows, 2 * HEAD_DIM), F32)]
        + [shape((n * rows, 2 * HEAD_DIM), BF16) for n in needs],
        [r, base, windows],
        [counted, held[0], *halo, *qg],
        scratch=[
            vmem((blocks * rows, HEAD_DIM), BF16),
            vmem((blocks * rows, HEAD_DIM), BF16),
            vmem((HEAD_DIM, blocks * rows), BF16),
            vmem((HEAD_DIM, blocks * rows), BF16),
            vmem((blocks * rows, HEAD_DIM), F32),
            vmem((blocks * rows, HEAD_DIM), F32),
            vmem((group, rows, 2 * width), BF16),
            vmem((group, rows, 2 * width), BF16),
            vmem((HEAD_DIM, HEAD_DIM), F32),
        ],
        flops=12 * group * heads * rows * (hops + 1) * rows * HEAD_DIM,
        nbytes=4 << 20,
        vmem=40 << 20,
    )
    od, own, parts = results[:group], results[group], results[group + 1 :]
    back = [shift(part, -group * (k + 1)) for k, part in enumerate(parts)]
    od = [od[0]] + [swap(od[j], j) for j in range(1, group)]
    dkv = call(
        functools.partial(add_kv_kernel, group, needs),
        [shape((rows, 2 * HEAD_DIM), BF16)] * group,
        [r],
        [own, *back],
        scratch=[vmem((group, rows, 2 * HEAD_DIM), BF16)],
    )
    dkv = [dkv[0]] + [swap(dkv[j], j) for j in range(1, group)]
    attended, grad_queries = call(
        functools.partial(unpack_kernel, group), [shape((rows, group * width), BF16)] * 2, [r], od
    )
    grad_keys, grad_values = call(
        functools.partial(unpack_kernel, group),
        [shape((rows, group * HEAD_DIM), BF16)] * 2,
        [r],
        dkv,
    )
    return attended, grad_queries, grad_keys, grad_values


def solution(mesh):
    rows = P(("dp", "ctx"), "head")
    tokens = P(("dp", "ctx"))
    return jax.shard_map(
        per_device,
        mesh=mesh,
        in_specs=(rows, rows, rows, rows, tokens, tokens, P("head")),
        out_specs=(rows, rows, rows, rows),
        check_vma=False,
    )
```

```python
import functools

import jax
import jax.numpy as jnp
from jax import lax
from jax.experimental import pallas as pl
from jax.experimental.pallas import tpu as pltpu
from jax.sharding import PartitionSpec as P

HEAD_DIM = 128
WINDOW = 768
AXIS = "ctx"
PAD = 16
PAIR = 2
BF16 = jnp.bfloat16
F32 = jnp.float32
NEG = -1e30
NT = (((1,), (1,)), ((), ()))
NN = (((1,), (0,)), ((), ()))


def dot(a, b, dims=NN):
    return lax.dot_general(a, b, dims, preferred_element_type=F32)


def block_at(index, size):
    return pl.ds(pl.multiple_of(index * size, size), size)


def call(
    kernel, out_shape, scalars, vectors, scratch=(), flops=0, nbytes=0, vmem=None, space=pltpu.VMEM
):
    def keep(array):
        return pltpu.with_memory_space_constraint(array, space) if space == pltpu.HBM else array

    return pl.pallas_call(
        kernel,
        out_shape=out_shape,
        in_specs=[pl.BlockSpec(memory_space=pltpu.SMEM)] * len(scalars)
        + [pl.BlockSpec(memory_space=space)] * len(vectors),
        out_specs=jax.tree.map(lambda _: pl.BlockSpec(memory_space=pltpu.VMEM), out_shape),
        scratch_shapes=list(scratch),
        cost_estimate=pl.CostEstimate(flops=flops, bytes_accessed=nbytes, transcendentals=0),
        compiler_params=pltpu.CompilerParams(vmem_limit_bytes=vmem),
    )(*scalars, *[keep(v) for v in vectors])


def pack_kv_kernel(group, r_ref, key_ref, value_ref, doc_ref, mask_ref, *refs):
    out_refs, (line_ref, sems) = refs[:group], refs[group:]
    r = r_ref[0]
    rows = key_ref.shape[0]
    copies = [
        pltpu.make_async_copy(doc_ref, line_ref.at[:, 0:HEAD_DIM], sems.at[0]),
        pltpu.make_async_copy(mask_ref, line_ref.at[:, HEAD_DIM:], sems.at[1]),
    ]
    for j in range(group):
        cols = block_at(r ^ j, HEAD_DIM)
        for i, ref in enumerate((key_ref, value_ref)):
            into = out_refs[j].at[0:rows, i * HEAD_DIM : (i + 1) * HEAD_DIM]
            copies.append(pltpu.make_async_copy(ref.at[:, cols], into, sems.at[2 + 2 * j + i]))
    for copy in copies:
        copy.start()
    for copy in copies[:2]:
        copy.wait()
    tail = jnp.broadcast_to(line_ref[...].astype(F32), (PAD, 2 * HEAD_DIM)).astype(BF16)
    for j in range(group):
        out_refs[j][rows:, :] = tail
    for copy in copies[2:]:
        copy.wait()


def pack_qg_kernel(group, r_ref, query_ref, grad_ref, *refs):
    out_refs, sems = refs[:group], refs[group]
    r = r_ref[0]
    width = query_ref.shape[1] // group
    copies = []
    for j in range(group):
        cols = block_at(r ^ j, width)
        for i, ref in enumerate((query_ref, grad_ref)):
            into = out_refs[j].at[:, i * width : (i + 1) * width]
            copies.append(pltpu.make_async_copy(ref.at[:, cols], into, sems.at[2 * j + i]))
    for copy in copies:
        copy.start()
    for copy in copies:
        copy.wait()


def encode_count(total):
    high = jnp.floor(total * (1.0 / 64.0))
    return jnp.concatenate([high, total - 64.0 * high], axis=1).astype(BF16)


def decode_count(line):
    line = line.astype(F32)
    return 64.0 * line[:, 0:HEAD_DIM] + line[:, HEAD_DIM:]


def gather_kernel(group, needs, r_ref, *refs):
    slots, outs = refs[:group], refs[group:]
    r = r_ref[0]
    full, count_ref = outs[0], outs[-1]
    rows = full.shape[1] - PAD
    total = jnp.zeros((1, HEAD_DIM), F32)
    for j in range(group):
        full[r ^ j] = slots[j][...]
        total = total + slots[j][rows : rows + 1, HEAD_DIM:].astype(F32)
    total = jnp.broadcast_to(jnp.sum(total, axis=1, keepdims=True), count_ref.shape)
    count_ref[...] = total
    full[0, rows + 8 :, :] = encode_count(total)
    for need, out in zip([n for n in needs if n < group], outs[1:-1]):
        out[...] = full[group - need :]
        out[0, rows + 8 :, :] = encode_count(total)


def ordered_pieces(needs, group, own_ref, halo_refs):
    pieces = []
    for need, ref in reversed(list(zip(needs, halo_refs))):
        pieces += [(ref, i) for i in range(need)]
    return pieces + [(own_ref, i) for i in range(group)]


def attention_kernel(
    group, needs, heads, token_count, counts_ride, where_ref, count_ref, other_ref, own_ref, *refs
):
    halo_refs, refs = refs[: len(needs)], refs[len(needs) :]
    qg_refs, refs = refs[:group], refs[group:]
    out_refs, refs = refs[:group], refs[group:]
    own_out, refs = refs[0], refs[1:]
    halo_outs, refs = refs[: len(needs)], refs[len(needs) :]
    keys, values, keys_t, values_t, dkeys, dvalues, qg, od, lines = refs
    r = where_ref[0]
    rows = own_ref.shape[1] - PAD
    hops = sum(needs)
    blocks = hops + group
    span = (hops + 1) * rows
    width = heads * HEAD_DIM
    scale = HEAD_DIM**-0.5
    exp_scale = scale * 1.4426950408889634
    lowest = jnp.maximum(hops * rows - where_ref[1], 0)

    pieces = ordered_pieces(needs, group, own_ref, halo_refs)
    lines[...] = jnp.zeros_like(lines)
    total = count_ref[...] + other_ref[...]
    if counts_ride:
        for ref in halo_refs:
            total = total + decode_count(ref[0, rows + 8 :, :])
    factor = token_count / jnp.maximum(total[0:1, :], 1.0)
    for kb, (ref, i) in enumerate(pieces):
        at = slice(kb * rows, (kb + 1) * rows)
        key, value = ref[i, 0:rows, 0:HEAD_DIM], ref[i, 0:rows, HEAD_DIM:]
        keys[at, :] = key
        values[at, :] = value
        keys_t[:, at] = key.T
        values_t[:, at] = value.T
        doc = ref[i, rows : rows + 1, 0:HEAD_DIM].astype(F32)
        if kb < hops:
            doc = jnp.where(kb * rows < lowest, -1.0, doc)
        else:
            s = kb - hops
            mask = ref[i, rows : rows + 1, HEAD_DIM:].astype(F32)
            lines[blocks + s : blocks + s + 1, :] = mask * factor
        lines[kb : kb + 1, :] = doc
    columns = lines[...].T
    dkeys[...] = jnp.zeros_like(dkeys)
    dvalues[...] = jnp.zeros_like(dvalues)
    for j in range(group):
        qg[r ^ j] = qg_refs[j][...]

    lane = lax.broadcasted_iota(jnp.int32, (1, rows), 1)
    pos = lax.broadcasted_iota(jnp.int32, (span, PAIR * rows), 0)
    diag = lax.broadcasted_iota(jnp.int32, (rows, PAIR * rows), 0)
    own_lane = jnp.concatenate([lane] * PAIR, axis=1)
    for s in range(group):
        at = slice(s * rows, s * rows + span)
        doc_row = lines[hops + s : hops + s + 1, :]
        start = jnp.zeros((1, rows), F32)
        for kb in range(s, s + hops + 1):
            before = jnp.where(columns[:, kb : kb + 1] < doc_row, 1.0, 0.0)
            start = start + jnp.sum(before, axis=0, keepdims=True)
        start = jnp.maximum(start.astype(jnp.int32), lowest - s * rows)
        cot_col = columns[:, blocks + s : blocks + s + 1]
        for h0 in range(0, heads, PAIR):
            hs = range(h0, h0 + PAIR)
            low = jnp.concatenate(
                [
                    jnp.maximum(start, hops * rows + 1 + lane - where_ref[2 + h])
                    for h in hs
                ],
                axis=1,
            )
            query = jnp.concatenate(
                [qg[s, :, h * HEAD_DIM : (h + 1) * HEAD_DIM] for h in hs], axis=0
            )
            cots = [
                qg[s, :, width + h * HEAD_DIM : width + (h + 1) * HEAD_DIM].astype(F32) * cot_col
                for h in hs
            ]
            cots = [c.astype(BF16) for c in cots]
            cot = jnp.concatenate(cots, axis=0)
            cot_t = jnp.concatenate([c.T for c in cots], axis=1).astype(F32)
            scores = dot(keys[at, :], query, NT)
            allowed = pos >= low
            scores = jnp.where(allowed, scores, NEG)
            last = jnp.where(diag <= own_lane, scores[hops * rows :], NEG)
            scores = jnp.concatenate([scores[: hops * rows], last], axis=0)
            row_max = jnp.max(scores, axis=0, keepdims=True)
            raised = jnp.exp2(scores * exp_scale - row_max * exp_scale)
            weights = raised * (1.0 / jnp.sum(raised, axis=0, keepdims=True))
            weights_low = weights.astype(BF16)
            output_t = dot(values_t[:, at], weights_low)
            row_dot = jnp.sum(cot_t * output_t, axis=0, keepdims=True)
            grad_prob = dot(values[at, :], cot, NT)
            grad_score = (weights * (grad_prob - row_dot)).astype(BF16)
            dvalues[at, :] += dot(weights_low, cot)
            dkeys[at, :] += dot(grad_score, query)
            grad_query_t = dot(keys_t[:, at], grad_score) * scale
            for i, h in enumerate(hs):
                cut = slice(i * rows, (i + 1) * rows)
                od[s, :, h * HEAD_DIM : (h + 1) * HEAD_DIM] = output_t[:, cut].T.astype(BF16)
                od[s, :, width + h * HEAD_DIM : width + (h + 1) * HEAD_DIM] = grad_query_t[
                    :, cut
                ].T.astype(BF16)

    for j in range(group):
        out_refs[j][...] = od[r ^ j]
    first = hops * rows
    own_out[:, 0:HEAD_DIM] = dkeys[first:, :]
    own_out[:, HEAD_DIM:] = dvalues[first:, :]
    for need, out in zip(needs, halo_outs):
        first -= need * rows
        out[:, 0:HEAD_DIM] = dkeys[first : first + need * rows, :].astype(BF16)
        out[:, HEAD_DIM:] = dvalues[first : first + need * rows, :].astype(BF16)


def add_kv_kernel(group, needs, r_ref, own_ref, *refs):
    halo_refs, out_refs, total = refs[: len(needs)], refs[len(needs) : -1], refs[-1]
    r = r_ref[0]
    rows = own_ref.shape[0] // group
    scale = HEAD_DIM**-0.5
    for s in range(group):
        part = own_ref[s * rows : (s + 1) * rows, :]
        for need, ref in zip(needs, halo_refs):
            i = s - (group - need)
            if i >= 0:
                part = part + ref[i * rows : (i + 1) * rows, :].astype(F32)
        total[s, :, 0:HEAD_DIM] = (part[:, 0:HEAD_DIM] * scale).astype(BF16)
        total[s, :, HEAD_DIM:] = part[:, HEAD_DIM:].astype(BF16)
    for j in range(group):
        out_refs[j][...] = total[r ^ j]


def unpack_kernel(group, r_ref, *refs):
    slots, (left_ref, right_ref) = refs[:group], refs[group:]
    r = r_ref[0]
    width = left_ref.shape[1] // group
    for j in range(group):
        cols = block_at(r ^ j, width)
        left_ref[:, cols] = slots[j][:, 0:width]
        right_ref[:, cols] = slots[j][:, width:]


def per_device(queries, key_rows, value_rows, grad_out, doc_ids, loss_mask, windows):
    count = lax.axis_size(AXIS)
    rows = key_rows.shape[0]
    group = key_rows.shape[1] // HEAD_DIM
    heads = queries.shape[1] // key_rows.shape[1]
    width = heads * HEAD_DIM
    assert rows == HEAD_DIM and count % group == 0 and group & (group - 1) == 0
    hops = (WINDOW - 1 + rows - 1) // rows
    needs = [min(group, hops - k) for k in range(0, hops, group)]
    blocks = hops + group
    span = (hops + 1) * rows
    index = lax.axis_index(AXIS)
    r = (index % group).reshape(1)
    base = ((index // group) * (group * rows)).reshape(1)
    where = jnp.concatenate([r, base, lax.dynamic_slice(windows, (r[0] * heads,), (heads,))])
    shape = jax.ShapeDtypeStruct
    vmem = pltpu.VMEM
    counts_ride = count == 4 * group and len(needs) == 2

    def swap(array, by):
        return lax.ppermute(array, AXIS, [(i, i ^ by) for i in range(count)])

    def shift(array, by, around):
        pairs = [(i, (i + by) % count) for i in range(count) if around or 0 <= i + by < count]
        return lax.ppermute(array, AXIS, pairs)

    message = shape((rows + PAD, 2 * HEAD_DIM), BF16)
    kv = call(
        functools.partial(pack_kv_kernel, group),
        [message] * group,
        [r],
        [key_rows, value_rows, doc_ids.reshape(1, rows), loss_mask.reshape(1, rows)],
        scratch=[
            vmem((1, 2 * HEAD_DIM), jnp.int32),
            pltpu.SemaphoreType.DMA((2 + 2 * group,)),
        ],
        vmem=4 << 20,
        space=pltpu.HBM,
    )
    kv = [kv[0]] + [swap(kv[j], j) for j in range(1, group)]
    qg = call(
        functools.partial(pack_qg_kernel, group),
        [shape((rows, 2 * width), BF16)] * group,
        [r],
        [queries, grad_out],
        scratch=[pltpu.SemaphoreType.DMA((2 * group,))],
        vmem=4 << 20,
        space=pltpu.HBM,
    )
    kv, where, _ = lax.optimization_barrier((kv, where, qg[0]))
    qg = [qg[0]] + [swap(qg[j], j) for j in range(1, group)]
    *held, counted = call(
        functools.partial(gather_kernel, group, needs),
        [shape((n, rows + PAD, 2 * HEAD_DIM), BF16) for n in [group] + [n for n in needs if n < group]]
        + [shape((8, HEAD_DIM), F32)],
        [r],
        kv,
        vmem=4 << 20,
    )
    parts = iter(held[1:])
    halo = [
        shift(held[0] if need == group else next(parts), group * (k + 1), counts_ride)
        for k, need in enumerate(needs)
    ]
    if counts_ride:
        others = shift(counted, -group, True)
    else:
        summed, by = counted, group
        while by < count:
            summed = summed + swap(summed, by)
            by *= 2
        others = summed - counted
    results = call(
        functools.partial(attention_kernel, group, needs, heads, float(count * rows), counts_ride),
        [shape((rows, 2 * width), BF16)] * group
        + [shape((group * rows, 2 * HEAD_DIM), F32)]
        + [shape((n * rows, 2 * HEAD_DIM), BF16) for n in needs],
        [where],
        [counted, others, held[0], *halo, *qg],
        scratch=[
            vmem((blocks * rows, HEAD_DIM), BF16),
            vmem((blocks * rows, HEAD_DIM), BF16),
            vmem((HEAD_DIM, blocks * rows), BF16),
            vmem((HEAD_DIM, blocks * rows), BF16),
            vmem((blocks * rows, HEAD_DIM), F32),
            vmem((blocks * rows, HEAD_DIM), F32),
            vmem((group, rows, 2 * width), BF16),
            vmem((group, rows, 2 * width), BF16),
            vmem((HEAD_DIM, HEAD_DIM), F32),
        ],
        flops=12 * group * heads * rows * span * HEAD_DIM,
        nbytes=4 << 20,
        vmem=24 << 20,
    )
    od, (own, *parts) = results[:group], results[group:]
    back = [shift(part, -group * (k + 1), False) for k, part in enumerate(parts)]
    od = [od[0]] + [swap(od[j], j) for j in range(1, group)]
    dkv = call(
        functools.partial(add_kv_kernel, group, needs),
        [shape((rows, 2 * HEAD_DIM), BF16)] * group,
        [r],
        [own, *back],
        scratch=[vmem((group, rows, 2 * HEAD_DIM), BF16)],
        vmem=4 << 20,
    )
    dkv = [dkv[0]] + [swap(dkv[j], j) for j in range(1, group)]
    attended, grad_queries = call(
        functools.partial(unpack_kernel, group),
        [shape((rows, group * width), BF16)] * 2,
        [r],
        od,
        vmem=4 << 20,
    )
    grad_keys, grad_values = call(
        functools.partial(unpack_kernel, group),
        [shape((rows, group * HEAD_DIM), BF16)] * 2,
        [r],
        dkv,
        vmem=4 << 20,
    )
    return attended, grad_queries, grad_keys, grad_values


def solution(mesh):
    rows = P(("dp", "ctx"), "head")
    tokens = P(("dp", "ctx"))
    return jax.shard_map(
        per_device,
        mesh=mesh,
        in_specs=(rows, rows, rows, rows, tokens, tokens, P("head")),
        out_specs=(rows, rows, rows, rows),
        check_vma=False,
    )
```

```python
import functools

import jax
import jax.numpy as jnp
from jax import lax
from jax.experimental import pallas as pl
from jax.experimental.pallas import tpu as pltpu
from jax.sharding import PartitionSpec as P

HEAD_DIM = 128
WINDOW = 768
AXIS = "ctx"
PAD = 16
PAIR = 2
BF16 = jnp.bfloat16
F32 = jnp.float32
NEG = -1e30
NT = (((1,), (1,)), ((), ()))
NN = (((1,), (0,)), ((), ()))


def dot(a, b, dims=NN):
    return lax.dot_general(a, b, dims, preferred_element_type=F32)


def block_at(index, size):
    return pl.ds(pl.multiple_of(index * size, size), size)


def call(
    kernel, out_shape, scalars, vectors, scratch=(), flops=0, nbytes=0, vmem=None, space=pltpu.VMEM
):
    def keep(array):
        return pltpu.with_memory_space_constraint(array, space) if space == pltpu.HBM else array

    return pl.pallas_call(
        kernel,
        out_shape=out_shape,
        in_specs=[pl.BlockSpec(memory_space=pltpu.SMEM)] * len(scalars)
        + [pl.BlockSpec(memory_space=space)] * len(vectors),
        out_specs=jax.tree.map(lambda _: pl.BlockSpec(memory_space=pltpu.VMEM), out_shape),
        scratch_shapes=list(scratch),
        cost_estimate=pl.CostEstimate(flops=flops, bytes_accessed=nbytes, transcendentals=0),
        compiler_params=pltpu.CompilerParams(vmem_limit_bytes=vmem),
    )(*scalars, *[keep(v) for v in vectors])


def pack_kv_kernel(group, r_ref, key_ref, value_ref, doc_ref, mask_ref, *refs):
    out_refs, (line_ref, sems) = refs[:group], refs[group:]
    r = r_ref[0]
    rows = key_ref.shape[0]
    copies = [
        pltpu.make_async_copy(doc_ref, line_ref.at[:, 0:HEAD_DIM], sems.at[0]),
        pltpu.make_async_copy(mask_ref, line_ref.at[:, HEAD_DIM:], sems.at[1]),
    ]
    for j in range(group):
        cols = block_at(r ^ j, HEAD_DIM)
        for i, ref in enumerate((key_ref, value_ref)):
            into = out_refs[j].at[0:rows, i * HEAD_DIM : (i + 1) * HEAD_DIM]
            copies.append(pltpu.make_async_copy(ref.at[:, cols], into, sems.at[2 + 2 * j + i]))
    for copy in copies:
        copy.start()
    for copy in copies[:2]:
        copy.wait()
    tail = jnp.broadcast_to(line_ref[...].astype(F32), (PAD, 2 * HEAD_DIM)).astype(BF16)
    for j in range(group):
        out_refs[j][rows:, :] = tail
    for copy in copies[2:]:
        copy.wait()


def pack_qg_kernel(group, r_ref, query_ref, grad_ref, *refs):
    out_refs, sems = refs[:group], refs[group]
    r = r_ref[0]
    width = query_ref.shape[1] // group
    copies = []
    for j in range(group):
        cols = block_at(r ^ j, width)
        for i, ref in enumerate((query_ref, grad_ref)):
            into = out_refs[j].at[:, i * width : (i + 1) * width]
            copies.append(pltpu.make_async_copy(ref.at[:, cols], into, sems.at[2 * j + i]))
    for copy in copies:
        copy.start()
    for copy in copies:
        copy.wait()


def encode_count(total):
    high = jnp.floor(total * (1.0 / 64.0))
    return jnp.concatenate([high, total - 64.0 * high], axis=1).astype(BF16)


def decode_count(line):
    line = line.astype(F32)
    return 64.0 * line[:, 0:HEAD_DIM] + line[:, HEAD_DIM:]


def gather_kernel(group, r_ref, *refs):
    slots, (parts, count_ref, full) = refs[:group], (refs[group:-2], *refs[-2:])
    r = r_ref[0]
    rows = full.shape[1] - PAD
    total = jnp.zeros((1, HEAD_DIM), F32)
    for j in range(group):
        full[r ^ j] = slots[j][...]
        total = total + slots[j][rows : rows + 1, HEAD_DIM:].astype(F32)
    total = jnp.broadcast_to(jnp.sum(total, axis=1, keepdims=True), count_ref.shape)
    count_ref[...] = total
    first = 0
    for part in parts:
        part[...] = full[first : first + part.shape[0]]
        first += part.shape[0]
    parts[-1][0, rows + 8 :, :] = encode_count(total)


def relay_kernel(part_ref, got_ref, out_ref):
    out_ref[...] = (part_ref[...] + got_ref[...].astype(F32)).astype(BF16)


def attention_kernel(
    group, sizes, links, heads, token_count, counts_ride, where_ref, count_ref, other_ref, *refs
):
    shards = range(group)
    hops = sum(sizes) - group
    part_refs, refs = refs[: len(sizes)], refs[len(sizes) :]
    qg_refs, refs = refs[:group], refs[group:]
    out_refs, own_out, refs = refs[:group], refs[group], refs[group + 1 :]
    sum_refs, (dkeys, dvalues, od, *refs) = refs[:-9], refs[-9:]
    keys, values, keys_t, values_t, qg, lines = refs
    r = where_ref[0]
    rows = qg_refs[0].shape[0]
    blocks = hops + group
    span = (hops + 1) * rows
    width = heads * HEAD_DIM
    scale = HEAD_DIM**-0.5
    exp_scale = scale * 1.4426950408889634
    lowest = jnp.maximum(hops * rows - where_ref[1], 0)

    lines[...] = jnp.zeros_like(lines)
    total = count_ref[...] + other_ref[...]
    if counts_ride:
        for i in links:
            total = total + decode_count(part_refs[i][0, rows + 8 :, :])
    factor = token_count / jnp.maximum(total[0:1, :], 1.0)
    pieces = [(ref, i) for ref in part_refs for i in range(ref.shape[0])]
    for kb, (ref, i) in enumerate(pieces):
        at = slice(kb * rows, (kb + 1) * rows)
        key, value = ref[i, 0:rows, 0:HEAD_DIM], ref[i, 0:rows, HEAD_DIM:]
        keys[at, :] = key
        values[at, :] = value
        keys_t[:, at] = key.T
        values_t[:, at] = value.T
        doc = ref[i, rows : rows + 1, 0:HEAD_DIM].astype(F32)
        if kb < hops:
            doc = jnp.where(kb * rows < lowest, -1.0, doc)
        else:
            mask = ref[i, rows : rows + 1, HEAD_DIM:].astype(F32)
            lines[blocks + kb - hops : blocks + kb - hops + 1, :] = mask * factor
        lines[kb : kb + 1, :] = doc
    columns = lines[...].T
    dkeys[...] = jnp.zeros_like(dkeys)
    dvalues[...] = jnp.zeros_like(dvalues)
    for j in range(group):
        qg[r ^ j] = qg_refs[j][...]

    lane = lax.broadcasted_iota(jnp.int32, (1, rows), 1)
    pos = lax.broadcasted_iota(jnp.int32, (span, PAIR * rows), 0)
    diag = lax.broadcasted_iota(jnp.int32, (rows, PAIR * rows), 0)
    own_lane = jnp.concatenate([lane] * PAIR, axis=1)
    starts = {}
    for s in shards:
        doc_row = lines[hops + s : hops + s + 1, :]
        start = jnp.zeros((1, rows), F32)
        for kb in range(s, s + hops + 1):
            before = jnp.where(columns[:, kb : kb + 1] < doc_row, 1.0, 0.0)
            start = start + jnp.sum(before, axis=0, keepdims=True)
        starts[s] = jnp.maximum(start.astype(jnp.int32), lowest - s * rows)
    steps = [(s, h0) for s in shards for h0 in range(0, heads, PAIR)]

    def head(part, s, h):
        return qg[s, :, part * width + h * HEAD_DIM : part * width + (h + 1) * HEAD_DIM]

    def products(s, h0):
        at = slice(s * rows, s * rows + span)
        hs = range(h0, h0 + PAIR)
        query = jnp.concatenate([head(0, s, h) for h in hs], axis=0)
        cot_col = columns[:, blocks + s : blocks + s + 1]
        cots = [(head(1, s, h).astype(F32) * cot_col).astype(BF16) for h in hs]
        cot = jnp.concatenate(cots, axis=0)
        cot_t = jnp.concatenate([c.T for c in cots], axis=1).astype(F32)
        scores = dot(keys[at, :], query, NT)
        return query, cot, cot_t, scores

    def softmax(s, h0, scores):
        hs = range(h0, h0 + PAIR)
        low = jnp.concatenate(
            [jnp.maximum(starts[s], hops * rows + 1 + lane - where_ref[2 + h]) for h in hs],
            axis=1,
        )
        scores = jnp.where(pos >= low, scores, NEG)
        last = jnp.where(diag <= own_lane, scores[hops * rows :], NEG)
        scores = jnp.concatenate([scores[: hops * rows], last], axis=0)
        row_max = jnp.max(scores, axis=0, keepdims=True)
        raised = jnp.exp2(scores * exp_scale - row_max * exp_scale)
        return raised * (1.0 / jnp.sum(raised, axis=0, keepdims=True))

    def finish(s, h0, query, cot, cot_t, weights):
        at = slice(s * rows, s * rows + span)
        weights_low = weights.astype(BF16)
        output_t = dot(values_t[:, at], weights_low)
        row_dot = jnp.sum(cot_t * output_t, axis=0, keepdims=True)
        grad_prob = dot(values[at, :], cot, NT)
        grad_score = (weights * (grad_prob - row_dot)).astype(BF16)
        dvalues[at, :] += dot(weights_low, cot)
        dkeys[at, :] += dot(grad_score, query)
        grad_query_t = dot(keys_t[:, at], grad_score) * scale
        for i in range(PAIR):
            h = h0 + i
            cut = slice(i * rows, (i + 1) * rows)
            od[s, :, h * HEAD_DIM : (h + 1) * HEAD_DIM] = output_t[:, cut].T.astype(BF16)
            od[s, :, width + h * HEAD_DIM : width + (h + 1) * HEAD_DIM] = grad_query_t[
                :, cut
            ].T.astype(BF16)

    ahead = products(*steps[0])
    for i, step in enumerate(steps):
        query, cot, cot_t, scores = ahead
        if i + 1 < len(steps):
            ahead = products(*steps[i + 1])
        finish(*step, query, cot, cot_t, softmax(*step, scores))

    for j in range(group):
        out_refs[j][...] = od[r ^ j]
    edge = hops * rows
    own_out[:, 0:HEAD_DIM] = dkeys[edge:, :]
    own_out[:, HEAD_DIM:] = dvalues[edge:, :]
    edge = 0
    for out in sum_refs:
        at = slice(edge, edge + out.shape[0])
        out[:, 0:HEAD_DIM] = dkeys[at, :].astype(out.dtype)
        out[:, HEAD_DIM:] = dvalues[at, :].astype(out.dtype)
        edge += out.shape[0]


def add_kv_kernel(group, firsts, r_ref, own_ref, *refs):
    got_refs, out_refs, total = refs[: len(firsts)], refs[len(firsts) : -1], refs[-1]
    r = r_ref[0]
    rows = own_ref.shape[0] // group
    scale = HEAD_DIM**-0.5
    for s in range(group):
        part = own_ref[s * rows : (s + 1) * rows, :]
        for first, ref in zip(firsts, got_refs):
            i = s - first
            if 0 <= i < ref.shape[0] // rows:
                part = part + ref[i * rows : (i + 1) * rows, :].astype(F32)
        total[s, :, 0:HEAD_DIM] = (part[:, 0:HEAD_DIM] * scale).astype(BF16)
        total[s, :, HEAD_DIM:] = part[:, HEAD_DIM:].astype(BF16)
    for j in range(group):
        out_refs[j][...] = total[r ^ j]


def unpack_kernel(group, r_ref, *refs):
    slots, (left_ref, right_ref) = refs[:group], refs[group:]
    r = r_ref[0]
    width = left_ref.shape[1] // group
    for j in range(group):
        cols = block_at(r ^ j, width)
        left_ref[:, cols] = slots[j][:, 0:width]
        right_ref[:, cols] = slots[j][:, width:]


def per_device(queries, key_rows, value_rows, grad_out, doc_ids, loss_mask, windows):
    count = lax.axis_size(AXIS)
    rows = key_rows.shape[0]
    group = key_rows.shape[1] // HEAD_DIM
    heads = queries.shape[1] // key_rows.shape[1]
    width = heads * HEAD_DIM
    assert rows == HEAD_DIM and count % group == 0 and group & (group - 1) == 0
    hops = (WINDOW - 1 + rows - 1) // rows
    needs = [min(group, hops - k) for k in range(0, hops, group)]
    blocks = hops + group
    span = (hops + 1) * rows
    index = lax.axis_index(AXIS)
    r = (index % group).reshape(1)
    base = ((index // group) * (group * rows)).reshape(1)
    where = jnp.concatenate([r, base, lax.dynamic_slice(windows, (r[0] * heads,), (heads,))])
    shape = jax.ShapeDtypeStruct
    vmem = pltpu.VMEM
    counts_ride = count == 4 * group and len(needs) == 2

    def swap(array, by):
        return lax.ppermute(array, AXIS, [(i, i ^ by) for i in range(count)])

    def shift(array, by, around):
        pairs = [(i, (i + by) % count) for i in range(count) if around or 0 <= i + by < count]
        return lax.ppermute(array, AXIS, pairs)

    message = shape((rows + PAD, 2 * HEAD_DIM), BF16)
    kv = call(
        functools.partial(pack_kv_kernel, group),
        [message] * group,
        [r],
        [key_rows, value_rows, doc_ids.reshape(1, rows), loss_mask.reshape(1, rows)],
        scratch=[
            vmem((1, 2 * HEAD_DIM), jnp.int32),
            pltpu.SemaphoreType.DMA((2 + 2 * group,)),
        ],
        vmem=4 << 20,
        space=pltpu.HBM,
    )
    kv = [kv[0]] + [swap(kv[j], j) for j in range(1, group)]
    qg = call(
        functools.partial(pack_qg_kernel, group),
        [shape((rows, 2 * width), BF16)] * group,
        [r],
        [queries, grad_out],
        scratch=[pltpu.SemaphoreType.DMA((2 * group,))],
        vmem=4 << 20,
        space=pltpu.HBM,
    )
    kv, where, _ = lax.optimization_barrier((kv, where, qg[0]))
    qg = [qg[0]] + [swap(qg[j], j) for j in range(1, group)]

    chain = needs[-1]
    rest = group - chain
    own_sizes = [rest, chain] if rest else [chain]
    *held, counted = call(
        functools.partial(gather_kernel, group),
        [shape((n, rows + PAD, 2 * HEAD_DIM), BF16) for n in own_sizes]
        + [shape((8, HEAD_DIM), F32)],
        [r],
        kv,
        scratch=[vmem((group, rows + PAD, 2 * HEAD_DIM), BF16)],
        vmem=4 << 20,
    )
    parts, sizes, links = list(held), list(own_sizes), []
    passed = held[-1]
    for k, need in enumerate(needs):
        passed = shift(passed, group, counts_ride)
        before = [passed]
        if need > chain:
            before = [shift(held[0], group * (k + 1), False), passed]
        parts, sizes = before + parts, [need - chain] * (need > chain) + [chain] + sizes
        links = [len(before) - 1] + [i + len(before) for i in links]
    if counts_ride:
        parts[links[-1]], late = lax.optimization_barrier((parts[links[-1]], counted))
        others = shift(late, -group, True)
    else:
        summed, by = counted, group
        while by < count:
            summed = summed + swap(summed, by)
            by *= 2
        others = summed - counted

    sums = (blocks * rows, HEAD_DIM)
    stack = (group, rows, 2 * width)
    halo_sizes = sizes[: -len(own_sizes)]
    results = call(
        functools.partial(
            attention_kernel, group, sizes, links, heads, float(count * rows), counts_ride
        ),
        [shape((rows, 2 * width), BF16)] * group
        + [shape((group * rows, 2 * HEAD_DIM), F32)]
        + [
            shape((n * rows, 2 * HEAD_DIM), F32 if i in links[1:] else BF16)
            for i, n in enumerate(halo_sizes)
        ],
        [where],
        [counted, others, *parts, *qg],
        scratch=[
            vmem(sums, F32),
            vmem(sums, F32),
            vmem(stack, BF16),
            vmem(sums, BF16),
            vmem(sums, BF16),
            vmem(sums[::-1], BF16),
            vmem(sums[::-1], BF16),
            vmem(stack, BF16),
            vmem((HEAD_DIM, HEAD_DIM), F32),
        ],
        flops=12 * group * heads * rows * span * HEAD_DIM,
        nbytes=16 << 20,
        vmem=24 << 20,
    )
    od, (own, *partial) = results[:group], results[group:]
    passed = shift(partial[links[0]], -group, False)
    for i in links[1:]:
        passed = call(relay_kernel, shape(passed.shape, BF16), [], [partial[i], passed], vmem=2 << 20)
        passed = shift(passed, -group, False)
    firsts, back = [rest], [passed]
    for k, i in enumerate(links[::-1]):
        if needs[k] > chain:
            firsts.append(0)
            back.append(shift(partial[i - 1], -group * (k + 1), False))
    od = [od[0]] + [swap(od[j], j) for j in range(1, group)]
    dkv = call(
        functools.partial(add_kv_kernel, group, firsts),
        [shape((rows, 2 * HEAD_DIM), BF16)] * group,
        [r],
        [own, *back],
        scratch=[vmem((group, rows, 2 * HEAD_DIM), BF16)],
        vmem=4 << 20,
    )
    dkv = [dkv[0]] + [swap(dkv[j], j) for j in range(1, group)]
    attended, grad_queries = call(
        functools.partial(unpack_kernel, group),
        [shape((rows, group * width), BF16)] * 2,
        [r],
        od,
        vmem=4 << 20,
    )
    grad_keys, grad_values = call(
        functools.partial(unpack_kernel, group),
        [shape((rows, group * HEAD_DIM), BF16)] * 2,
        [r],
        dkv,
        vmem=4 << 20,
    )
    return attended, grad_queries, grad_keys, grad_values


def solution(mesh):
    rows = P(("dp", "ctx"), "head")
    tokens = P(("dp", "ctx"))
    return jax.shard_map(
        per_device,
        mesh=mesh,
        in_specs=(rows, rows, rows, rows, tokens, tokens, P("head")),
        out_specs=(rows, rows, rows, rows),
        check_vma=False,
    )
```

```python
import functools

import jax
import jax.numpy as jnp
from jax import lax
from jax.experimental import pallas as pl
from jax.experimental.pallas import tpu as pltpu
from jax.sharding import PartitionSpec as P

HEAD_DIM = 128
WINDOW = 768
AXIS = "ctx"
PAD = 16
PAIR = 2
BF16 = jnp.bfloat16
F32 = jnp.float32
NEG = -1e30
NT = (((1,), (1,)), ((), ()))
NN = (((1,), (0,)), ((), ()))


def dot(a, b, dims=NN):
    return lax.dot_general(a, b, dims, preferred_element_type=F32)


def block_at(index, size):
    return pl.ds(pl.multiple_of(index * size, size), size)


def call(
    kernel, out_shape, scalars, vectors, scratch=(), flops=0, nbytes=0, vmem=None, space=pltpu.VMEM
):
    def keep(array):
        return pltpu.with_memory_space_constraint(array, space) if space == pltpu.HBM else array

    return pl.pallas_call(
        kernel,
        out_shape=out_shape,
        in_specs=[pl.BlockSpec(memory_space=pltpu.SMEM)] * len(scalars)
        + [pl.BlockSpec(memory_space=space)] * len(vectors),
        out_specs=jax.tree.map(lambda _: pl.BlockSpec(memory_space=pltpu.VMEM), out_shape),
        scratch_shapes=list(scratch),
        cost_estimate=pl.CostEstimate(flops=flops, bytes_accessed=nbytes, transcendentals=0),
        compiler_params=pltpu.CompilerParams(vmem_limit_bytes=vmem),
    )(*scalars, *[keep(v) for v in vectors])


def pack_kv_kernel(group, r_ref, key_ref, value_ref, doc_ref, mask_ref, *refs):
    out_refs, (line_ref, sems) = refs[:group], refs[group:]
    r = r_ref[0]
    rows = key_ref.shape[0]
    copies = [
        pltpu.make_async_copy(doc_ref, line_ref.at[:, 0:HEAD_DIM], sems.at[0]),
        pltpu.make_async_copy(mask_ref, line_ref.at[:, HEAD_DIM:], sems.at[1]),
    ]
    for j in range(group):
        cols = block_at(r ^ j, HEAD_DIM)
        for i, ref in enumerate((key_ref, value_ref)):
            into = out_refs[j].at[0:rows, i * HEAD_DIM : (i + 1) * HEAD_DIM]
            copies.append(pltpu.make_async_copy(ref.at[:, cols], into, sems.at[2 + 2 * j + i]))
    for copy in copies:
        copy.start()
    for copy in copies[:2]:
        copy.wait()
    tail = jnp.broadcast_to(line_ref[...].astype(F32), (PAD, 2 * HEAD_DIM)).astype(BF16)
    for j in range(group):
        out_refs[j][rows:, :] = tail
    for copy in copies[2:]:
        copy.wait()


def pack_qg_kernel(group, r_ref, query_ref, grad_ref, *refs):
    out_refs, sems = refs[:group], refs[group]
    r = r_ref[0]
    rows, width = query_ref.shape[0], query_ref.shape[1] // group
    copies = []
    for j in range(group):
        cols = block_at(r ^ j, width)
        for i, ref in enumerate((query_ref, grad_ref)):
            into = out_refs[j].at[0:rows, i * width : (i + 1) * width]
            copies.append(pltpu.make_async_copy(ref.at[:, cols], into, sems.at[2 * j + i]))
    for copy in copies:
        copy.start()
    for copy in copies:
        copy.wait()


def encode_count(total):
    high = jnp.floor(total * (1.0 / 64.0))
    return jnp.concatenate([high, total - 64.0 * high], axis=1)


def decode_count(line):
    line = line.astype(F32)
    return 64.0 * line[:, 0:HEAD_DIM] + line[:, HEAD_DIM:]


def gather_kernel(group, r_ref, *refs):
    slots, (part, count_ref, full, lines) = refs[:group], refs[group:]
    r = r_ref[0]
    rows = full.shape[1]
    lines[...] = jnp.zeros_like(lines)
    for j in range(group):
        full[r ^ j] = slots[j][0:rows, :]
        lines[pl.ds(r ^ j, 1), :] = slots[j][rows : rows + 1, :].astype(F32)
    total = jnp.sum(jnp.sum(lines[:, HEAD_DIM:], axis=0, keepdims=True), axis=1, keepdims=True)
    total = jnp.broadcast_to(total, count_ref.shape)
    count_ref[...] = total
    for s in range(group):
        part[s * rows : (s + 1) * rows, :] = full[s]
    tail = jnp.concatenate([lines[...], encode_count(total)], axis=0)
    part[group * rows :, :] = tail.astype(BF16)


def cut_kernel(skip, part_ref, out_ref):
    rows = HEAD_DIM
    size = out_ref.shape[0] - PAD
    out_ref[0:size, :] = part_ref[skip * rows : skip * rows + size, :]
    tail = part_ref[skip * rows + size :, :].astype(F32)
    tail = jnp.concatenate([tail[skip : PAD // 2], tail[:skip], tail[PAD // 2 :]], axis=0)
    out_ref[size:, :] = tail.astype(BF16)


def count_kernel(count_ref, near_ref, out_ref):
    out_ref[...] = count_ref[...] + decode_count(near_ref[near_ref.shape[0] - PAD // 2 :, :])


def relay_kernel(part_ref, got_ref, out_ref):
    got = got_ref[0 : part_ref.shape[0], :].astype(F32)
    out_ref[...] = (part_ref[...] + got).astype(BF16)


def attention_kernel(
    group, sizes, heads, token_count, others, near_count, where_ref, count_ref, *refs
):
    shards = range(group)
    hops = sum(sizes) - group
    other_refs, refs = refs[:others], refs[others:]
    part_refs, refs = refs[: len(sizes)], refs[len(sizes) :]
    qg_refs, refs = refs[:group], refs[group:]
    out_refs, own_out, refs = refs[:group], refs[group], refs[group + 1 :]
    sum_refs, (dkeys, dvalues, od, *refs) = refs[:-9], refs[-9:]
    keys, values, keys_t, values_t, qg, lines = refs
    r = where_ref[0]
    rows = lines.shape[0]
    blocks = hops + group
    span = (hops + 1) * rows
    width = heads * HEAD_DIM
    scale = HEAD_DIM**-0.5
    exp_scale = scale * 1.4426950408889634
    lowest = jnp.maximum(hops * rows - where_ref[1], 0)

    lines[...] = jnp.zeros_like(lines)
    total = count_ref[...]
    for ref in other_refs:
        total = total + ref[...]
    if near_count:
        near = part_refs[-2]
        total = total + decode_count(near[near.shape[0] - PAD // 2 :, :])
    factor = token_count / jnp.maximum(total[0:1, :], 1.0)
    pieces = [(ref, n, i) for ref, n in zip(part_refs, sizes) for i in range(n)]
    for kb, (ref, n, i) in enumerate(pieces):
        at = slice(kb * rows, (kb + 1) * rows)
        piece = ref[i * rows : (i + 1) * rows, :]
        key, value = piece[:, 0:HEAD_DIM], piece[:, HEAD_DIM:]
        line = ref[n * rows : n * rows + PAD // 2, :].astype(F32)[i : i + 1, :]
        keys[at, :] = key
        values[at, :] = value
        keys_t[:, at] = key.T
        values_t[:, at] = value.T
        doc = line[:, 0:HEAD_DIM]
        if kb < hops:
            doc = jnp.where(kb * rows < lowest, -1.0, doc)
        else:
            lines[blocks + kb - hops : blocks + kb - hops + 1, :] = line[:, HEAD_DIM:] * factor
        lines[kb : kb + 1, :] = doc
    columns = lines[...].T
    dkeys[...] = jnp.zeros_like(dkeys)
    dvalues[...] = jnp.zeros_like(dvalues)
    for j in range(group):
        qg[r ^ j] = qg_refs[j][0:rows, :]

    lane = lax.broadcasted_iota(jnp.int32, (1, rows), 1)
    pos = lax.broadcasted_iota(jnp.int32, (span, PAIR * rows), 0)
    diag = lax.broadcasted_iota(jnp.int32, (rows, PAIR * rows), 0)
    own_lane = jnp.concatenate([lane] * PAIR, axis=1)
    starts = {}
    for s in shards:
        doc_row = lines[hops + s : hops + s + 1, :]
        start = jnp.zeros((1, rows), F32)
        for kb in range(s, s + hops + 1):
            before = jnp.where(columns[:, kb : kb + 1] < doc_row, 1.0, 0.0)
            start = start + jnp.sum(before, axis=0, keepdims=True)
        starts[s] = jnp.maximum(start.astype(jnp.int32), lowest - s * rows)
    steps = [(s, h0) for s in shards for h0 in range(0, heads, PAIR)]

    def head(part, s, h):
        return qg[s, :, part * width + h * HEAD_DIM : part * width + (h + 1) * HEAD_DIM]

    def products(s, h0):
        at = slice(s * rows, s * rows + span)
        hs = range(h0, h0 + PAIR)
        query = jnp.concatenate([head(0, s, h) for h in hs], axis=0)
        cot_col = columns[:, blocks + s : blocks + s + 1]
        cots = [(head(1, s, h).astype(F32) * cot_col).astype(BF16) for h in hs]
        cot = jnp.concatenate(cots, axis=0)
        cot_t = jnp.concatenate([c.T for c in cots], axis=1).astype(F32)
        scores = dot(keys[at, :], query, NT)
        return query, cot, cot_t, scores

    def softmax(s, h0, scores):
        hs = range(h0, h0 + PAIR)
        low = jnp.concatenate(
            [jnp.maximum(starts[s], hops * rows + 1 + lane - where_ref[2 + h]) for h in hs],
            axis=1,
        )
        scores = jnp.where(pos >= low, scores, NEG)
        last = jnp.where(diag <= own_lane, scores[hops * rows :], NEG)
        scores = jnp.concatenate([scores[: hops * rows], last], axis=0)
        row_max = jnp.max(scores, axis=0, keepdims=True)
        raised = jnp.exp2(scores * exp_scale - row_max * exp_scale)
        return raised * (1.0 / jnp.sum(raised, axis=0, keepdims=True))

    def finish(s, h0, query, cot, cot_t, weights):
        at = slice(s * rows, s * rows + span)
        weights_low = weights.astype(BF16)
        output_t = dot(values_t[:, at], weights_low)
        row_dot = jnp.sum(cot_t * output_t, axis=0, keepdims=True)
        grad_prob = dot(values[at, :], cot, NT)
        grad_score = (weights * (grad_prob - row_dot)).astype(BF16)
        dvalues[at, :] += dot(weights_low, cot)
        dkeys[at, :] += dot(grad_score, query)
        grad_query_t = dot(keys_t[:, at], grad_score) * scale
        for i in range(PAIR):
            h = h0 + i
            cut = slice(i * rows, (i + 1) * rows)
            od[s, :, h * HEAD_DIM : (h + 1) * HEAD_DIM] = output_t[:, cut].T.astype(BF16)
            od[s, :, width + h * HEAD_DIM : width + (h + 1) * HEAD_DIM] = grad_query_t[
                :, cut
            ].T.astype(BF16)

    ahead = products(*steps[0])
    for i, step in enumerate(steps):
        query, cot, cot_t, scores = ahead
        if i + 1 < len(steps):
            ahead = products(*steps[i + 1])
        finish(*step, query, cot, cot_t, softmax(*step, scores))

    for j in range(group):
        out_refs[j][...] = od[r ^ j]
    edge = hops * rows
    own_out[:, 0:HEAD_DIM] = dkeys[edge:, :]
    own_out[:, HEAD_DIM:] = dvalues[edge:, :]
    edge = 0
    for out in sum_refs:
        at = slice(edge, edge + out.shape[0])
        out[:, 0:HEAD_DIM] = dkeys[at, :].astype(out.dtype)
        out[:, HEAD_DIM:] = dvalues[at, :].astype(out.dtype)
        edge += out.shape[0]


def add_kv_kernel(group, firsts, r_ref, own_ref, *refs):
    got_refs, out_refs, total = refs[: len(firsts)], refs[len(firsts) : -1], refs[-1]
    r = r_ref[0]
    rows = own_ref.shape[0] // group
    scale = HEAD_DIM**-0.5
    for s in range(group):
        part = own_ref[s * rows : (s + 1) * rows, :]
        for first, ref in zip(firsts, got_refs):
            i = s - first
            if 0 <= i < ref.shape[0] // rows:
                part = part + ref[i * rows : (i + 1) * rows, :].astype(F32)
        total[s, :, 0:HEAD_DIM] = (part[:, 0:HEAD_DIM] * scale).astype(BF16)
        total[s, :, HEAD_DIM:] = part[:, HEAD_DIM:].astype(BF16)
    for j in range(group):
        out_refs[j][...] = total[r ^ j]


def unpack_kernel(group, r_ref, *refs):
    slots, (left_ref, right_ref) = refs[:group], refs[group:]
    r = r_ref[0]
    width = left_ref.shape[1] // group
    for j in range(group):
        cols = block_at(r ^ j, width)
        left_ref[:, cols] = slots[j][:, 0:width]
        right_ref[:, cols] = slots[j][:, width:]


def per_device(queries, key_rows, value_rows, grad_out, doc_ids, loss_mask, windows):
    count = lax.axis_size(AXIS)
    rows = key_rows.shape[0]
    group = key_rows.shape[1] // HEAD_DIM
    heads = queries.shape[1] // key_rows.shape[1]
    width = heads * HEAD_DIM
    assert rows == HEAD_DIM and count % group == 0 and group & (group - 1) == 0
    hops = (WINDOW - 1 + rows - 1) // rows
    needs = [min(group, hops - k) for k in range(0, hops, group)]
    blocks = hops + group
    span = (hops + 1) * rows
    index = lax.axis_index(AXIS)
    r = (index % group).reshape(1)
    base = ((index // group) * (group * rows)).reshape(1)
    where = jnp.concatenate([r, base, lax.dynamic_slice(windows, (r[0] * heads,), (heads,))])
    shape = jax.ShapeDtypeStruct
    vmem = pltpu.VMEM
    near_count = count == 4 * group and group > 1

    def swap(array, by):
        return lax.ppermute(array, AXIS, [(i, i ^ by) for i in range(count)])

    def shift(array, by, around=False):
        pairs = [(i, (i + by) % count) for i in range(count) if around or 0 <= i + by < count]
        return lax.ppermute(array, AXIS, pairs)

    message = shape((rows + PAD, 2 * HEAD_DIM), BF16)
    kv = call(
        functools.partial(pack_kv_kernel, group),
        [message] * group,
        [r],
        [key_rows, value_rows, doc_ids.reshape(1, rows), loss_mask.reshape(1, rows)],
        scratch=[
            vmem((1, 2 * HEAD_DIM), jnp.int32),
            pltpu.SemaphoreType.DMA((2 + 2 * group,)),
        ],
        vmem=4 << 20,
        space=pltpu.HBM,
    )
    kv = [kv[0]] + [swap(kv[j], j) for j in range(1, group)]
    qg = call(
        functools.partial(pack_qg_kernel, group),
        [shape((rows, 2 * width), BF16)] * group,
        [r],
        [queries, grad_out],
        scratch=[pltpu.SemaphoreType.DMA((2 * group,))],
        vmem=4 << 20,
        space=pltpu.HBM,
    )
    kv, where, _ = lax.optimization_barrier((kv, where, qg[0]))
    qg = [qg[0]] + [swap(qg[j], j) for j in range(1, group)]

    held, counted = call(
        functools.partial(gather_kernel, group),
        [shape((group * rows + PAD, 2 * HEAD_DIM), BF16), shape((8, HEAD_DIM), F32)],
        [r],
        kv,
        scratch=[vmem((group, rows, 2 * HEAD_DIM), BF16), vmem((8, 2 * HEAD_DIM), F32)],
        vmem=4 << 20,
    )
    halo, passed, size = [], held, group
    for k, need in enumerate(needs):
        if need < size:
            passed = call(
                functools.partial(cut_kernel, size - need),
                shape((need * rows + PAD, 2 * HEAD_DIM), BF16),
                [],
                [passed],
                vmem=2 << 20,
            )
        passed, size = shift(passed, group, near_count and k == 0), need
        halo.append(passed)
    sizes = needs[::-1] + [group]
    if near_count:
        pair = call(count_kernel, shape(counted.shape, F32), [], [counted, halo[0]], vmem=1 << 20)
        others = [swap(pair, 2 * group)]
    else:
        others, by = [jnp.zeros_like(counted)], group
        while by < count:
            counted, others = counted + others[0], [swap(counted + others[0], by)]
            by *= 2

    sums = (blocks * rows, HEAD_DIM)
    stack = (group, rows, 2 * width)
    chain = needs[-1]
    joined = len(needs) == 2 and needs[0] > chain
    pieces, links = [], []
    for k, need in reversed(list(enumerate(needs))):
        if need > chain and joined:
            pieces[-1] = need
        elif need > chain:
            pieces.append(need - chain)
        pieces.append(chain)
        links.append(len(pieces) - 1)
    results = call(
        functools.partial(
            attention_kernel, group, sizes, heads, float(count * rows), len(others), near_count
        ),
        [shape((rows, 2 * width), BF16)] * group
        + [shape((group * rows, 2 * HEAD_DIM), F32)]
        + [
            shape((n * rows, 2 * HEAD_DIM), F32 if i in links[1:] else BF16)
            for i, n in enumerate(pieces)
        ],
        [where],
        [counted, *others, *halo[::-1], held, *qg],
        scratch=[
            vmem(sums, F32),
            vmem(sums, F32),
            vmem(stack, BF16),
            vmem(sums, BF16),
            vmem(sums, BF16),
            vmem(sums[::-1], BF16),
            vmem(sums[::-1], BF16),
            vmem(stack, BF16),
            vmem((HEAD_DIM, HEAD_DIM), F32),
        ],
        flops=12 * group * heads * rows * span * HEAD_DIM,
        nbytes=16 << 20,
        vmem=24 << 20,
    )
    od, (own, *partial) = results[:group], results[group:]
    firsts, back = [], []
    passed = shift(partial[links[0]], -group)
    if joined:
        firsts.append(-chain)
        back.append(passed)
    for i in links[1:]:
        passed = call(
            relay_kernel, shape((chain * rows, 2 * HEAD_DIM), BF16), [], [partial[i], passed], vmem=2 << 20
        )
        passed = shift(passed, -group)
    firsts.append(group - chain)
    back.append(passed)
    for k, i in enumerate(links[::-1]):
        if needs[k] > chain and not joined:
            firsts.append(0)
            back.append(shift(partial[i - 1], -group * (k + 1)))
    od = [od[0]] + [swap(od[j], j) for j in range(1, group)]
    dkv = call(
        functools.partial(add_kv_kernel, group, firsts),
        [shape((rows, 2 * HEAD_DIM), BF16)] * group,
        [r],
        [own, *back],
        scratch=[vmem((group, rows, 2 * HEAD_DIM), BF16)],
        vmem=4 << 20,
    )
    dkv = [dkv[0]] + [swap(dkv[j], j) for j in range(1, group)]
    attended, grad_queries = call(
        functools.partial(unpack_kernel, group),
        [shape((rows, group * width), BF16)] * 2,
        [r],
        od,
        vmem=4 << 20,
    )
    grad_keys, grad_values = call(
        functools.partial(unpack_kernel, group),
        [shape((rows, group * HEAD_DIM), BF16)] * 2,
        [r],
        dkv,
        vmem=4 << 20,
    )
    return attended, grad_queries, grad_keys, grad_values


def solution(mesh):
    rows = P(("dp", "ctx"), "head")
    tokens = P(("dp", "ctx"))
    return jax.shard_map(
        per_device,
        mesh=mesh,
        in_specs=(rows, rows, rows, rows, tokens, tokens, P("head")),
        out_specs=(rows, rows, rows, rows),
        check_vma=False,
    )
```

```python
import functools

import jax
import jax.numpy as jnp
from jax import lax
from jax.experimental import pallas as pl
from jax.experimental.pallas import tpu as pltpu
from jax.sharding import PartitionSpec as P

HEAD_DIM = 128
WINDOW = 768
AXIS = "ctx"
PAD = 16
PAIR = 2
BF16 = jnp.bfloat16
F32 = jnp.float32
NEG = -1e30
NT = (((1,), (1,)), ((), ()))
NN = (((1,), (0,)), ((), ()))


def dot(a, b, dims=NN):
    return lax.dot_general(a, b, dims, preferred_element_type=F32)


def block_at(index, size):
    return pl.ds(pl.multiple_of(index * size, size), size)


def call(
    kernel, out_shape, scalars, vectors, scratch=(), flops=0, nbytes=0, vmem=None, space=pltpu.VMEM
):
    def keep(array):
        return pltpu.with_memory_space_constraint(array, space) if space == pltpu.HBM else array

    return pl.pallas_call(
        kernel,
        out_shape=out_shape,
        in_specs=[pl.BlockSpec(memory_space=pltpu.SMEM)] * len(scalars)
        + [pl.BlockSpec(memory_space=space)] * len(vectors),
        out_specs=jax.tree.map(lambda _: pl.BlockSpec(memory_space=pltpu.VMEM), out_shape),
        scratch_shapes=list(scratch),
        cost_estimate=pl.CostEstimate(flops=flops, bytes_accessed=nbytes, transcendentals=0),
        compiler_params=pltpu.CompilerParams(vmem_limit_bytes=vmem),
    )(*scalars, *[keep(v) for v in vectors])


def pack_kv_kernel(group, r_ref, key_ref, value_ref, doc_ref, mask_ref, *refs):
    out_refs, (line_ref, sems) = refs[:group], refs[group:]
    r = r_ref[0]
    rows = key_ref.shape[0]
    copies = [
        pltpu.make_async_copy(doc_ref, line_ref.at[:, 0:HEAD_DIM], sems.at[0]),
        pltpu.make_async_copy(mask_ref, line_ref.at[:, HEAD_DIM:], sems.at[1]),
    ]
    for j in range(group):
        cols = block_at(r ^ j, HEAD_DIM)
        for i, ref in enumerate((key_ref, value_ref)):
            into = out_refs[j].at[0:rows, i * HEAD_DIM : (i + 1) * HEAD_DIM]
            copies.append(pltpu.make_async_copy(ref.at[:, cols], into, sems.at[2 + 2 * j + i]))
    for copy in copies:
        copy.start()
    for copy in copies[:2]:
        copy.wait()
    tail = jnp.broadcast_to(line_ref[...].astype(F32), (PAD, 2 * HEAD_DIM)).astype(BF16)
    for j in range(group):
        out_refs[j][rows:, :] = tail
    for copy in copies[2:]:
        copy.wait()


def pack_qg_kernel(group, r_ref, query_ref, grad_ref, *refs):
    out_refs, sems = refs[:group], refs[group]
    r = r_ref[0]
    rows, width = query_ref.shape[0], query_ref.shape[1] // group
    copies = []
    for j in range(group):
        cols = block_at(r ^ j, width)
        for i, ref in enumerate((query_ref, grad_ref)):
            into = out_refs[j].at[0:rows, i * width : (i + 1) * width]
            copies.append(pltpu.make_async_copy(ref.at[:, cols], into, sems.at[2 * j + i]))
    for copy in copies:
        copy.start()
    for copy in copies:
        copy.wait()


def encode_count(total):
    high = jnp.floor(total * (1.0 / 64.0))
    return jnp.concatenate([high, total - 64.0 * high], axis=1)


def decode_count(line):
    line = line.astype(F32)
    return 64.0 * line[:, 0:HEAD_DIM] + line[:, HEAD_DIM:]


def gather_kernel(group, r_ref, *refs):
    slots, (part, count_ref, full, lines) = refs[:group], refs[group:]
    r = r_ref[0]
    rows = full.shape[1]
    lines[...] = jnp.zeros_like(lines)
    for j in range(group):
        full[r ^ j] = slots[j][0:rows, :]
        lines[pl.ds(r ^ j, 1), :] = slots[j][rows : rows + 1, :].astype(F32)
    total = jnp.sum(jnp.sum(lines[:, HEAD_DIM:], axis=0, keepdims=True), axis=1, keepdims=True)
    total = jnp.broadcast_to(total, count_ref.shape)
    count_ref[...] = total
    for s in range(group):
        part[s * rows : (s + 1) * rows, :] = full[s]
    tail = jnp.concatenate([lines[...], encode_count(total)], axis=0)
    part[group * rows :, :] = tail.astype(BF16)


def cut_kernel(skip, part_ref, out_ref):
    rows = HEAD_DIM
    size = out_ref.shape[0] - PAD
    out_ref[0:size, :] = part_ref[skip * rows : skip * rows + size, :]
    tail = part_ref[skip * rows + size :, :].astype(F32)
    tail = jnp.concatenate([tail[skip : PAD // 2], tail[:skip], tail[PAD // 2 :]], axis=0)
    out_ref[size:, :] = tail.astype(BF16)


def count_kernel(count_ref, near_ref, out_ref):
    out_ref[...] = count_ref[...] + decode_count(near_ref[near_ref.shape[0] - PAD // 2 :, :])


def relay_kernel(part_ref, got_ref, out_ref):
    got = got_ref[0 : part_ref.shape[0], :].astype(F32)
    out_ref[...] = (part_ref[...] + got).astype(BF16)


def attention_kernel(
    group, sizes, heads, token_count, others, near_count, where_ref, count_ref, *refs
):
    shards = range(group)
    hops = sum(sizes) - group
    other_refs, refs = refs[:others], refs[others:]
    part_refs, refs = refs[: len(sizes)], refs[len(sizes) :]
    qg_refs, refs = refs[:group], refs[group:]
    out_refs, own_out, refs = refs[:group], refs[group], refs[group + 1 :]
    sum_refs, (dkeys, dvalues, od, *refs) = refs[:-9], refs[-9:]
    keys, values, keys_t, values_t, qg, lines = refs
    r = where_ref[0]
    rows = lines.shape[0]
    blocks = hops + group
    span = (hops + 1) * rows
    width = heads * HEAD_DIM
    scale = HEAD_DIM**-0.5
    exp_scale = scale * 1.4426950408889634
    lowest = jnp.maximum(hops * rows - where_ref[1], 0)

    lines[...] = jnp.zeros_like(lines)
    total = count_ref[...]
    for ref in other_refs:
        total = total + ref[...]
    if near_count:
        near = part_refs[-2]
        total = total + decode_count(near[near.shape[0] - PAD // 2 :, :])
    factor = token_count / jnp.maximum(total[0:1, :], 1.0)
    pieces = [(ref, n, i) for ref, n in zip(part_refs, sizes) for i in range(n)]
    for kb, (ref, n, i) in enumerate(pieces):
        at = slice(kb * rows, (kb + 1) * rows)
        piece = ref[i * rows : (i + 1) * rows, :]
        key, value = piece[:, 0:HEAD_DIM], piece[:, HEAD_DIM:]
        line = ref[n * rows : n * rows + PAD // 2, :].astype(F32)[i : i + 1, :]
        keys[at, :] = key
        values[at, :] = value
        keys_t[:, at] = key.T
        values_t[:, at] = value.T
        doc = line[:, 0:HEAD_DIM]
        if kb < hops:
            doc = jnp.where(kb * rows < lowest, -1.0, doc)
        else:
            lines[blocks + kb - hops : blocks + kb - hops + 1, :] = line[:, HEAD_DIM:] * factor
        lines[kb : kb + 1, :] = doc
    columns = lines[...].T
    dkeys[...] = jnp.zeros_like(dkeys)
    dvalues[...] = jnp.zeros_like(dvalues)
    for j in range(group):
        qg[r ^ j] = qg_refs[j][0:rows, :]

    lane = lax.broadcasted_iota(jnp.int32, (1, rows), 1)
    pos = lax.broadcasted_iota(jnp.int32, (span, PAIR * rows), 0)
    diag = lax.broadcasted_iota(jnp.int32, (rows, PAIR * rows), 0)
    own_lane = jnp.concatenate([lane] * PAIR, axis=1)
    starts = {}
    for s in shards:
        doc_row = lines[hops + s : hops + s + 1, :]
        start = jnp.zeros((1, rows), F32)
        for kb in range(s, s + hops + 1):
            before = jnp.where(columns[:, kb : kb + 1] < doc_row, 1.0, 0.0)
            start = start + jnp.sum(before, axis=0, keepdims=True)
        starts[s] = jnp.maximum(start.astype(jnp.int32), lowest - s * rows)
    steps = [(s, h0) for s in shards for h0 in range(0, heads, PAIR)]

    def head(part, s, h):
        return qg[s, :, part * width + h * HEAD_DIM : part * width + (h + 1) * HEAD_DIM]

    def products(s, h0):
        at = slice(s * rows, s * rows + span)
        hs = range(h0, h0 + PAIR)
        query = jnp.concatenate([head(0, s, h) for h in hs], axis=0)
        cot_col = columns[:, blocks + s : blocks + s + 1]
        cots = [(head(1, s, h).astype(F32) * cot_col).astype(BF16) for h in hs]
        cot = jnp.concatenate(cots, axis=0)
        cot_t = jnp.concatenate([c.T for c in cots], axis=1).astype(F32)
        scores = dot(keys[at, :], query, NT)
        return query, cot, cot_t, scores

    def softmax(s, h0, scores):
        hs = range(h0, h0 + PAIR)
        low = jnp.concatenate(
            [jnp.maximum(starts[s], hops * rows + 1 + lane - where_ref[2 + h]) for h in hs],
            axis=1,
        )
        scores = jnp.where(pos >= low, scores, NEG)
        last = jnp.where(diag <= own_lane, scores[hops * rows :], NEG)
        scores = jnp.concatenate([scores[: hops * rows], last], axis=0)
        row_max = jnp.max(scores, axis=0, keepdims=True)
        raised = jnp.exp2(scores * exp_scale - row_max * exp_scale)
        return raised * (1.0 / jnp.sum(raised, axis=0, keepdims=True))

    def finish(s, h0, query, cot, cot_t, weights):
        at = slice(s * rows, s * rows + span)
        weights_low = weights.astype(BF16)
        output_t = dot(values_t[:, at], weights_low)
        row_dot = jnp.sum(cot_t * output_t, axis=0, keepdims=True)
        grad_prob = dot(values[at, :], cot, NT)
        grad_score = (weights * (grad_prob - row_dot)).astype(BF16)
        dvalues[at, :] += dot(weights_low, cot)
        dkeys[at, :] += dot(grad_score, query)
        grad_query_t = dot(keys_t[:, at], grad_score) * scale
        for i in range(PAIR):
            h = h0 + i
            cut = slice(i * rows, (i + 1) * rows)
            od[s, :, h * HEAD_DIM : (h + 1) * HEAD_DIM] = output_t[:, cut].T.astype(BF16)
            od[s, :, width + h * HEAD_DIM : width + (h + 1) * HEAD_DIM] = grad_query_t[
                :, cut
            ].T.astype(BF16)

    ahead = products(*steps[0])
    for i, step in enumerate(steps):
        query, cot, cot_t, scores = ahead
        if i + 1 < len(steps):
            ahead = products(*steps[i + 1])
        finish(*step, query, cot, cot_t, softmax(*step, scores))

    for j in range(group):
        out_refs[j][...] = od[r ^ j]
    edge = hops * rows
    own_out[:, 0:HEAD_DIM] = dkeys[edge:, :]
    own_out[:, HEAD_DIM:] = dvalues[edge:, :]
    edge = 0
    for out in sum_refs:
        at = slice(edge, edge + out.shape[0])
        out[:, 0:HEAD_DIM] = dkeys[at, :].astype(out.dtype)
        out[:, HEAD_DIM:] = dvalues[at, :].astype(out.dtype)
        edge += out.shape[0]


def add_kv_kernel(group, firsts, r_ref, own_ref, *refs):
    got_refs, out_refs, total = refs[: len(firsts)], refs[len(firsts) : -1], refs[-1]
    r = r_ref[0]
    rows = own_ref.shape[0] // group
    scale = HEAD_DIM**-0.5
    for s in range(group):
        part = own_ref[s * rows : (s + 1) * rows, :]
        for first, ref in zip(firsts, got_refs):
            i = s - first
            if 0 <= i < ref.shape[0] // rows:
                part = part + ref[i * rows : (i + 1) * rows, :].astype(F32)
        total[s, :, 0:HEAD_DIM] = (part[:, 0:HEAD_DIM] * scale).astype(BF16)
        total[s, :, HEAD_DIM:] = part[:, HEAD_DIM:].astype(BF16)
    for j in range(group):
        out_refs[j][...] = total[r ^ j]


def unpack_kernel(group, r_ref, *refs):
    slots, (left_ref, right_ref) = refs[:group], refs[group:]
    r = r_ref[0]
    width = left_ref.shape[1] // group
    for j in range(group):
        cols = block_at(r ^ j, width)
        left_ref[:, cols] = slots[j][:, 0:width]
        right_ref[:, cols] = slots[j][:, width:]


def per_device(queries, key_rows, value_rows, grad_out, doc_ids, loss_mask, windows):
    count = lax.axis_size(AXIS)
    rows = key_rows.shape[0]
    group = key_rows.shape[1] // HEAD_DIM
    heads = queries.shape[1] // key_rows.shape[1]
    width = heads * HEAD_DIM
    assert rows == HEAD_DIM and count % group == 0 and group & (group - 1) == 0
    hops = (WINDOW - 1 + rows - 1) // rows
    needs = [min(group, hops - k) for k in range(0, hops, group)]
    blocks = hops + group
    span = (hops + 1) * rows
    index = lax.axis_index(AXIS)
    r = (index % group).reshape(1)
    base = ((index // group) * (group * rows)).reshape(1)
    where = jnp.concatenate([r, base, lax.dynamic_slice(windows, (r[0] * heads,), (heads,))])
    shape = jax.ShapeDtypeStruct
    vmem = pltpu.VMEM
    near_count = count == 4 * group and group > 1

    def swap(array, by):
        return lax.ppermute(array, AXIS, [(i, i ^ by) for i in range(count)])

    def swap_all(slots):
        got = {j: swap(slots[j], j) for j in range(group - 1, 0, -1)}
        return [slots[0]] + [got[j] for j in range(1, group)]

    def shift(array, by, around=False):
        pairs = [(i, (i + by) % count) for i in range(count) if around or 0 <= i + by < count]
        return lax.ppermute(array, AXIS, pairs)

    message = shape((rows + PAD, 2 * HEAD_DIM), BF16)
    kv = call(
        functools.partial(pack_kv_kernel, group),
        [message] * group,
        [r],
        [key_rows, value_rows, doc_ids.reshape(1, rows), loss_mask.reshape(1, rows)],
        scratch=[
            vmem((1, 2 * HEAD_DIM), jnp.int32),
            pltpu.SemaphoreType.DMA((2 + 2 * group,)),
        ],
        vmem=4 << 20,
        space=pltpu.HBM,
    )
    kv = swap_all(kv)
    qg = call(
        functools.partial(pack_qg_kernel, group),
        [shape((rows, 2 * width), BF16)] * group,
        [r],
        [queries, grad_out],
        scratch=[pltpu.SemaphoreType.DMA((2 * group,))],
        vmem=4 << 20,
        space=pltpu.HBM,
    )
    kv, where, _ = lax.optimization_barrier((kv, where, qg[0]))
    qg = swap_all(qg)

    held, counted = call(
        functools.partial(gather_kernel, group),
        [shape((group * rows + PAD, 2 * HEAD_DIM), BF16), shape((8, HEAD_DIM), F32)],
        [r],
        kv,
        scratch=[vmem((group, rows, 2 * HEAD_DIM), BF16), vmem((8, 2 * HEAD_DIM), F32)],
        vmem=4 << 20,
    )
    halo, passed, size = [], held, group
    for k, need in enumerate(needs):
        if need < size:
            passed = call(
                functools.partial(cut_kernel, size - need),
                shape((need * rows + PAD, 2 * HEAD_DIM), BF16),
                [],
                [passed],
                vmem=2 << 20,
            )
        passed, size = shift(passed, group, near_count and k == 0), need
        halo.append(passed)
    sizes = needs[::-1] + [group]
    if near_count:
        pair = call(count_kernel, shape(counted.shape, F32), [], [counted, halo[0]], vmem=1 << 20)
        others = [swap(pair, 2 * group)]
    else:
        others, by = [jnp.zeros_like(counted)], group
        while by < count:
            counted, others = counted + others[0], [swap(counted + others[0], by)]
            by *= 2

    sums = (blocks * rows, HEAD_DIM)
    stack = (group, rows, 2 * width)
    chain = needs[-1]
    joined = len(needs) == 2 and needs[0] > chain
    pieces, links = [], []
    for k, need in reversed(list(enumerate(needs))):
        if need > chain and joined:
            pieces[-1] = need
        elif need > chain:
            pieces.append(need - chain)
        pieces.append(chain)
        links.append(len(pieces) - 1)
    results = call(
        functools.partial(
            attention_kernel, group, sizes, heads, float(count * rows), len(others), near_count
        ),
        [shape((rows, 2 * width), BF16)] * group
        + [shape((group * rows, 2 * HEAD_DIM), F32)]
        + [
            shape((n * rows, 2 * HEAD_DIM), F32 if i in links[1:] else BF16)
            for i, n in enumerate(pieces)
        ],
        [where],
        [counted, *others, *halo[::-1], held, *qg],
        scratch=[
            vmem(sums, F32),
            vmem(sums, F32),
            vmem(stack, BF16),
            vmem(sums, BF16),
            vmem(sums, BF16),
            vmem(sums[::-1], BF16),
            vmem(sums[::-1], BF16),
            vmem(stack, BF16),
            vmem((HEAD_DIM, HEAD_DIM), F32),
        ],
        flops=12 * group * heads * rows * span * HEAD_DIM,
        nbytes=16 << 20,
        vmem=24 << 20,
    )
    od, (own, *partial) = results[:group], results[group:]
    firsts, back = [], []
    passed = shift(partial[links[0]], -group, True)
    if joined:
        firsts.append(-chain)
        back.append(passed)
    for i in links[1:]:
        passed = call(
            relay_kernel, shape((chain * rows, 2 * HEAD_DIM), BF16), [], [partial[i], passed], vmem=2 << 20
        )
        passed = shift(passed, -group, True)
    firsts.append(group - chain)
    back.append(passed)
    for k, i in enumerate(links[::-1]):
        if needs[k] > chain and not joined:
            firsts.append(0)
            back.append(shift(partial[i - 1], -group * (k + 1)))
    od = swap_all(od)
    dkv = call(
        functools.partial(add_kv_kernel, group, firsts),
        [shape((rows, 2 * HEAD_DIM), BF16)] * group,
        [r],
        [own, *back],
        scratch=[vmem((group, rows, 2 * HEAD_DIM), BF16)],
        vmem=4 << 20,
    )
    dkv = swap_all(dkv)
    attended, grad_queries = call(
        functools.partial(unpack_kernel, group),
        [shape((rows, group * width), BF16)] * 2,
        [r],
        od,
        vmem=4 << 20,
    )
    grad_keys, grad_values = call(
        functools.partial(unpack_kernel, group),
        [shape((rows, group * HEAD_DIM), BF16)] * 2,
        [r],
        dkv,
        vmem=4 << 20,
    )
    return attended, grad_queries, grad_keys, grad_values


def solution(mesh):
    rows = P(("dp", "ctx"), "head")
    tokens = P(("dp", "ctx"))
    return jax.shard_map(
        per_device,
        mesh=mesh,
        in_specs=(rows, rows, rows, rows, tokens, tokens, P("head")),
        out_specs=(rows, rows, rows, rows),
        check_vma=False,
    )
```

```python
import functools

import jax
import jax.numpy as jnp
from jax import lax
from jax.experimental import pallas as pl
from jax.experimental.pallas import tpu as pltpu
from jax.sharding import PartitionSpec as P

HEAD_DIM = 128
WINDOW = 768
AXIS = "ctx"
PAD = 16
PAIR = 2
BF16 = jnp.bfloat16
F32 = jnp.float32
NEG = -1e30
NT = (((1,), (1,)), ((), ()))
NN = (((1,), (0,)), ((), ()))


def dot(a, b, dims=NN):
    return lax.dot_general(a, b, dims, preferred_element_type=F32)


def block_at(index, size):
    return pl.ds(pl.multiple_of(index * size, size), size)


def call(
    kernel, out_shape, scalars, vectors, scratch=(), flops=0, nbytes=0, vmem=None, space=pltpu.VMEM, into=pltpu.VMEM
):
    def keep(array):
        return pltpu.with_memory_space_constraint(array, space) if space == pltpu.HBM else array

    return pl.pallas_call(
        kernel,
        out_shape=out_shape,
        in_specs=[pl.BlockSpec(memory_space=pltpu.SMEM)] * len(scalars)
        + [pl.BlockSpec(memory_space=space)] * len(vectors),
        out_specs=jax.tree.map(lambda _: pl.BlockSpec(memory_space=into), out_shape),
        scratch_shapes=list(scratch),
        cost_estimate=pl.CostEstimate(flops=flops, bytes_accessed=nbytes, transcendentals=0),
        compiler_params=pltpu.CompilerParams(vmem_limit_bytes=vmem),
    )(*scalars, *[keep(v) for v in vectors])


def pack_kv_kernel(group, r_ref, key_ref, value_ref, doc_ref, mask_ref, *refs):
    out_refs, (line_ref, sems) = refs[:group], refs[group:]
    r = r_ref[0]
    rows = key_ref.shape[0]
    copies = [
        pltpu.make_async_copy(doc_ref, line_ref.at[:, 0:HEAD_DIM], sems.at[0]),
        pltpu.make_async_copy(mask_ref, line_ref.at[:, HEAD_DIM:], sems.at[1]),
    ]
    for j in range(group):
        cols = block_at(r ^ j, HEAD_DIM)
        for i, ref in enumerate((key_ref, value_ref)):
            into = out_refs[j].at[0:rows, i * HEAD_DIM : (i + 1) * HEAD_DIM]
            copies.append(pltpu.make_async_copy(ref.at[:, cols], into, sems.at[2 + 2 * j + i]))
    for copy in copies:
        copy.start()
    for copy in copies[:2]:
        copy.wait()
    tail = jnp.broadcast_to(line_ref[...].astype(F32), (PAD, 2 * HEAD_DIM)).astype(BF16)
    for j in range(group):
        out_refs[j][rows:, :] = tail
    for copy in copies[2:]:
        copy.wait()


def pack_qg_kernel(group, r_ref, query_ref, grad_ref, *refs):
    out_refs, sems = refs[:group], refs[group]
    r = r_ref[0]
    rows, width = query_ref.shape[0], query_ref.shape[1] // group
    copies = []
    for j in range(group):
        cols = block_at(r ^ j, width)
        for i, ref in enumerate((query_ref, grad_ref)):
            into = out_refs[j].at[0:rows, i * width : (i + 1) * width]
            copies.append(pltpu.make_async_copy(ref.at[:, cols], into, sems.at[2 * j + i]))
    for copy in copies:
        copy.start()
    for copy in copies:
        copy.wait()


def encode_count(total):
    high = jnp.floor(total * (1.0 / 64.0))
    return jnp.concatenate([high, total - 64.0 * high], axis=1)


def decode_count(line):
    line = line.astype(F32)
    return 64.0 * line[:, 0:HEAD_DIM] + line[:, HEAD_DIM:]


def gather_kernel(group, r_ref, *refs):
    slots, (part, count_ref, full, lines) = refs[:group], refs[group:]
    r = r_ref[0]
    rows = full.shape[1]
    lines[...] = jnp.zeros_like(lines)
    for j in range(group):
        full[r ^ j] = slots[j][0:rows, :]
        lines[pl.ds(r ^ j, 1), :] = slots[j][rows : rows + 1, :].astype(F32)
    total = jnp.sum(jnp.sum(lines[:, HEAD_DIM:], axis=0, keepdims=True), axis=1, keepdims=True)
    total = jnp.broadcast_to(total, count_ref.shape)
    count_ref[...] = total
    for s in range(group):
        part[s * rows : (s + 1) * rows, :] = full[s]
    tail = jnp.concatenate([lines[...], encode_count(total)], axis=0)
    part[group * rows :, :] = tail.astype(BF16)


def cut_kernel(skip, part_ref, out_ref):
    rows = HEAD_DIM
    size = out_ref.shape[0] - PAD
    out_ref[0:size, :] = part_ref[skip * rows : skip * rows + size, :]
    tail = part_ref[skip * rows + size :, :].astype(F32)
    tail = jnp.concatenate([tail[skip : PAD // 2], tail[:skip], tail[PAD // 2 :]], axis=0)
    out_ref[size:, :] = tail.astype(BF16)


def count_kernel(count_ref, near_ref, out_ref):
    out_ref[...] = count_ref[...] + decode_count(near_ref[near_ref.shape[0] - PAD // 2 :, :])


def relay_kernel(part_ref, got_ref, out_ref):
    got = got_ref[0 : part_ref.shape[0], :].astype(F32)
    out_ref[...] = (part_ref[...] + got).astype(BF16)


def attention_kernel(
    group, sizes, heads, token_count, others, near_count, where_ref, count_ref, *refs
):
    shards = range(group)
    hops = sum(sizes) - group
    other_refs, refs = refs[:others], refs[others:]
    part_refs, refs = refs[: len(sizes)], refs[len(sizes) :]
    qg_refs, refs = refs[:group], refs[group:]
    out_refs, own_out, refs = refs[:group], refs[group], refs[group + 1 :]
    sum_refs, (dkeys, dvalues, od, *refs) = refs[:-9], refs[-9:]
    keys, values, keys_t, values_t, qg, lines = refs
    r = where_ref[0]
    rows = lines.shape[0]
    blocks = hops + group
    span = (hops + 1) * rows
    width = heads * HEAD_DIM
    scale = HEAD_DIM**-0.5
    exp_scale = scale * 1.4426950408889634
    lowest = jnp.maximum(hops * rows - where_ref[1], 0)

    lines[...] = jnp.zeros_like(lines)
    total = count_ref[...]
    for ref in other_refs:
        total = total + ref[...]
    if near_count:
        near = part_refs[-2]
        total = total + decode_count(near[near.shape[0] - PAD // 2 :, :])
    factor = token_count / jnp.maximum(total[0:1, :], 1.0)
    pieces = [(ref, n, i) for ref, n in zip(part_refs, sizes) for i in range(n)]
    for kb, (ref, n, i) in enumerate(pieces):
        at = slice(kb * rows, (kb + 1) * rows)
        piece = ref[i * rows : (i + 1) * rows, :]
        key, value = piece[:, 0:HEAD_DIM], piece[:, HEAD_DIM:]
        line = ref[n * rows : n * rows + PAD // 2, :].astype(F32)[i : i + 1, :]
        keys[at, :] = key
        values[at, :] = value
        keys_t[:, at] = key.T
        values_t[:, at] = value.T
        doc = line[:, 0:HEAD_DIM]
        if kb < hops:
            doc = jnp.where(kb * rows < lowest, -1.0, doc)
        else:
            lines[blocks + kb - hops : blocks + kb - hops + 1, :] = line[:, HEAD_DIM:] * factor
        lines[kb : kb + 1, :] = doc
    columns = lines[...].T
    dkeys[...] = jnp.zeros_like(dkeys)
    dvalues[...] = jnp.zeros_like(dvalues)
    for j in range(group):
        qg[r ^ j] = qg_refs[j][0:rows, :]

    lane = lax.broadcasted_iota(jnp.int32, (1, rows), 1)
    pos = lax.broadcasted_iota(jnp.int32, (span, PAIR * rows), 0)
    diag = lax.broadcasted_iota(jnp.int32, (rows, PAIR * rows), 0)
    own_lane = jnp.concatenate([lane] * PAIR, axis=1)
    starts = {}
    for s in shards:
        doc_row = lines[hops + s : hops + s + 1, :]
        start = jnp.zeros((1, rows), F32)
        for kb in range(s, s + hops + 1):
            before = jnp.where(columns[:, kb : kb + 1] < doc_row, 1.0, 0.0)
            start = start + jnp.sum(before, axis=0, keepdims=True)
        starts[s] = jnp.maximum(start.astype(jnp.int32), lowest - s * rows)
    steps = [(s, h0) for s in shards for h0 in range(0, heads, PAIR)]

    def head(part, s, h):
        return qg[s, :, part * width + h * HEAD_DIM : part * width + (h + 1) * HEAD_DIM]

    def products(s, h0):
        at = slice(s * rows, s * rows + span)
        hs = range(h0, h0 + PAIR)
        query = jnp.concatenate([head(0, s, h) for h in hs], axis=0)
        cot_col = columns[:, blocks + s : blocks + s + 1]
        cots = [(head(1, s, h).astype(F32) * cot_col).astype(BF16) for h in hs]
        cot = jnp.concatenate(cots, axis=0)
        cot_t = jnp.concatenate([c.T for c in cots], axis=1).astype(F32)
        scores = dot(keys[at, :], query, NT)
        return query, cot, cot_t, scores

    def softmax(s, h0, scores):
        hs = range(h0, h0 + PAIR)
        low = jnp.concatenate(
            [jnp.maximum(starts[s], hops * rows + 1 + lane - where_ref[2 + h]) for h in hs],
            axis=1,
        )
        scores = jnp.where(pos >= low, scores, NEG)
        last = jnp.where(diag <= own_lane, scores[hops * rows :], NEG)
        scores = jnp.concatenate([scores[: hops * rows], last], axis=0)
        row_max = jnp.max(scores, axis=0, keepdims=True)
        raised = jnp.exp2(scores * exp_scale - row_max * exp_scale)
        return raised * (1.0 / jnp.sum(raised, axis=0, keepdims=True))

    def finish(s, h0, query, cot, cot_t, weights):
        at = slice(s * rows, s * rows + span)
        weights_low = weights.astype(BF16)
        output_t = dot(values_t[:, at], weights_low)
        row_dot = jnp.sum(cot_t * output_t, axis=0, keepdims=True)
        grad_prob = dot(values[at, :], cot, NT)
        grad_score = (weights * (grad_prob - row_dot)).astype(BF16)
        dvalues[at, :] += dot(weights_low, cot)
        dkeys[at, :] += dot(grad_score, query)
        grad_query_t = dot(keys_t[:, at], grad_score) * scale
        for i in range(PAIR):
            h = h0 + i
            cut = slice(i * rows, (i + 1) * rows)
            od[s, :, h * HEAD_DIM : (h + 1) * HEAD_DIM] = output_t[:, cut].T.astype(BF16)
            od[s, :, width + h * HEAD_DIM : width + (h + 1) * HEAD_DIM] = grad_query_t[
                :, cut
            ].T.astype(BF16)

    ahead = products(*steps[0])
    for i, step in enumerate(steps):
        query, cot, cot_t, scores = ahead
        if i + 1 < len(steps):
            ahead = products(*steps[i + 1])
        finish(*step, query, cot, cot_t, softmax(*step, scores))

    for j in range(group):
        out_refs[j][...] = od[r ^ j]
    edge = hops * rows
    own_out[:, 0:HEAD_DIM] = dkeys[edge:, :]
    own_out[:, HEAD_DIM:] = dvalues[edge:, :]
    edge = 0
    for out in sum_refs:
        at = slice(edge, edge + out.shape[0])
        out[:, 0:HEAD_DIM] = dkeys[at, :].astype(out.dtype)
        out[:, HEAD_DIM:] = dvalues[at, :].astype(out.dtype)
        edge += out.shape[0]


def add_kv_kernel(group, firsts, r_ref, own_ref, *refs):
    got_refs, out_refs, total = refs[: len(firsts)], refs[len(firsts) : -1], refs[-1]
    r = r_ref[0]
    rows = own_ref.shape[0] // group
    scale = HEAD_DIM**-0.5
    for s in range(group):
        part = own_ref[s * rows : (s + 1) * rows, :]
        for first, ref in zip(firsts, got_refs):
            i = s - first
            if 0 <= i < ref.shape[0] // rows:
                part = part + ref[i * rows : (i + 1) * rows, :].astype(F32)
        total[s, :, 0:HEAD_DIM] = (part[:, 0:HEAD_DIM] * scale).astype(BF16)
        total[s, :, HEAD_DIM:] = part[:, HEAD_DIM:].astype(BF16)
    for j in range(group):
        out_refs[j][...] = total[r ^ j]


def unpack_kernel(group, r_ref, *refs):
    slots, (left_ref, right_ref, sems) = refs[:group], refs[group:]
    r = r_ref[0]
    width = left_ref.shape[1] // group
    copies = []
    for j in range(group):
        cols = block_at(r ^ j, width)
        for i, ref in enumerate((left_ref, right_ref)):
            part = slots[j].at[:, i * width : (i + 1) * width]
            copies.append(pltpu.make_async_copy(part, ref.at[:, cols], sems.at[2 * j + i]))
    for copy in copies:
        copy.start()
    for copy in copies:
        copy.wait()


def per_device(queries, key_rows, value_rows, grad_out, doc_ids, loss_mask, windows):
    count = lax.axis_size(AXIS)
    rows = key_rows.shape[0]
    group = key_rows.shape[1] // HEAD_DIM
    heads = queries.shape[1] // key_rows.shape[1]
    width = heads * HEAD_DIM
    assert rows == HEAD_DIM and count % group == 0 and group & (group - 1) == 0
    hops = (WINDOW - 1 + rows - 1) // rows
    needs = [min(group, hops - k) for k in range(0, hops, group)]
    blocks = hops + group
    span = (hops + 1) * rows
    index = lax.axis_index(AXIS)
    r = (index % group).reshape(1)
    base = ((index // group) * (group * rows)).reshape(1)
    where = jnp.concatenate([r, base, lax.dynamic_slice(windows, (r[0] * heads,), (heads,))])
    shape = jax.ShapeDtypeStruct
    vmem = pltpu.VMEM
    near_count = count == 4 * group and group > 1

    def swap(array, by):
        return lax.ppermute(array, AXIS, [(i, i ^ by) for i in range(count)])

    def swap_all(slots):
        got = {j: swap(slots[j], j) for j in range(group - 1, 0, -1)}
        return [slots[0]] + [got[j] for j in range(1, group)]

    def shift(array, by, around=False):
        pairs = [(i, (i + by) % count) for i in range(count) if around or 0 <= i + by < count]
        return lax.ppermute(array, AXIS, pairs)

    message = shape((rows + PAD, 2 * HEAD_DIM), BF16)
    kv = call(
        functools.partial(pack_kv_kernel, group),
        [message] * group,
        [r],
        [key_rows, value_rows, doc_ids.reshape(1, rows), loss_mask.reshape(1, rows)],
        scratch=[
            vmem((1, 2 * HEAD_DIM), jnp.int32),
            pltpu.SemaphoreType.DMA((2 + 2 * group,)),
        ],
        vmem=4 << 20,
        space=pltpu.HBM,
    )
    kv = swap_all(kv)
    qg = call(
        functools.partial(pack_qg_kernel, group),
        [shape((rows, 2 * width), BF16)] * group,
        [r],
        [queries, grad_out],
        scratch=[pltpu.SemaphoreType.DMA((2 * group,))],
        vmem=4 << 20,
        space=pltpu.HBM,
    )
    kv, where, _ = lax.optimization_barrier((kv, where, qg[0]))
    qg = swap_all(qg)

    held, counted = call(
        functools.partial(gather_kernel, group),
        [shape((group * rows + PAD, 2 * HEAD_DIM), BF16), shape((8, HEAD_DIM), F32)],
        [r],
        kv,
        scratch=[vmem((group, rows, 2 * HEAD_DIM), BF16), vmem((8, 2 * HEAD_DIM), F32)],
        vmem=4 << 20,
    )
    halo, passed, size = [], held, group
    for k, need in enumerate(needs):
        if need < size:
            passed = call(
                functools.partial(cut_kernel, size - need),
                shape((need * rows + PAD, 2 * HEAD_DIM), BF16),
                [],
                [passed],
                vmem=2 << 20,
            )
        passed, size = shift(passed, group, near_count and k == 0), need
        halo.append(passed)
    sizes = needs[::-1] + [group]
    if near_count:
        pair = call(count_kernel, shape(counted.shape, F32), [], [counted, halo[0]], vmem=1 << 20)
        others = [swap(pair, 2 * group)]
    else:
        others, by = [jnp.zeros_like(counted)], group
        while by < count:
            counted, others = counted + others[0], [swap(counted + others[0], by)]
            by *= 2

    sums = (blocks * rows, HEAD_DIM)
    stack = (group, rows, 2 * width)
    chain = needs[-1]
    joined = len(needs) == 2 and needs[0] > chain
    pieces, links = [], []
    for k, need in reversed(list(enumerate(needs))):
        if need > chain and joined:
            pieces[-1] = need
        elif need > chain:
            pieces.append(need - chain)
        pieces.append(chain)
        links.append(len(pieces) - 1)
    results = call(
        functools.partial(
            attention_kernel, group, sizes, heads, float(count * rows), len(others), near_count
        ),
        [shape((rows, 2 * width), BF16)] * group
        + [shape((group * rows, 2 * HEAD_DIM), F32)]
        + [
            shape((n * rows, 2 * HEAD_DIM), F32 if i in links[1:] else BF16)
            for i, n in enumerate(pieces)
        ],
        [where],
        [counted, *others, *halo[::-1], held, *qg],
        scratch=[
            vmem(sums, F32),
            vmem(sums, F32),
            vmem(stack, BF16),
            vmem(sums, BF16),
            vmem(sums, BF16),
            vmem(sums[::-1], BF16),
            vmem(sums[::-1], BF16),
            vmem(stack, BF16),
            vmem((HEAD_DIM, HEAD_DIM), F32),
        ],
        flops=12 * group * heads * rows * span * HEAD_DIM,
        nbytes=16 << 20,
        vmem=24 << 20,
    )
    od, (own, *partial) = results[:group], results[group:]
    firsts, back = [], []
    passed = shift(partial[links[0]], -group, True)
    if joined:
        firsts.append(-chain)
        back.append(passed)
    for i in links[1:]:
        passed = call(
            relay_kernel, shape((chain * rows, 2 * HEAD_DIM), BF16), [], [partial[i], passed], vmem=2 << 20
        )
        passed = shift(passed, -group, True)
    firsts.append(group - chain)
    back.append(passed)
    for k, i in enumerate(links[::-1]):
        if needs[k] > chain and not joined:
            firsts.append(0)
            back.append(shift(partial[i - 1], -group * (k + 1)))
    od = swap_all(od)
    dkv = call(
        functools.partial(add_kv_kernel, group, firsts),
        [shape((rows, 2 * HEAD_DIM), BF16)] * group,
        [r],
        [own, *back],
        scratch=[vmem((group, rows, 2 * HEAD_DIM), BF16)],
        vmem=4 << 20,
    )
    dkv = swap_all(dkv)
    attended, grad_queries = call(
        functools.partial(unpack_kernel, group),
        [shape((rows, group * width), BF16)] * 2,
        [r],
        od,
        scratch=[pltpu.SemaphoreType.DMA((2 * group,))],
        vmem=4 << 20,
        into=pltpu.HBM,
    )
    grad_keys, grad_values = call(
        functools.partial(unpack_kernel, group),
        [shape((rows, group * HEAD_DIM), BF16)] * 2,
        [r],
        dkv,
        scratch=[pltpu.SemaphoreType.DMA((2 * group,))],
        vmem=4 << 20,
        into=pltpu.HBM,
    )
    return attended, grad_queries, grad_keys, grad_values


def solution(mesh):
    rows = P(("dp", "ctx"), "head")
    tokens = P(("dp", "ctx"))
    return jax.shard_map(
        per_device,
        mesh=mesh,
        in_specs=(rows, rows, rows, rows, tokens, tokens, P("head")),
        out_specs=(rows, rows, rows, rows),
        check_vma=False,
    )
```
